256 devices in a mesh: col: 32 (over y, z), disp: 8 (over x, core).
Axes of the slice: x: 4, y: 4, z: 8, core: 2. Of those that a mesh axis runs over, the one named last changes fastest.
Arguments:
- left: bfloat16 [320, 256, 128], P(None, 'col'), may hold values from -6 to 6
- right: bfloat16 [320, 256, 128], P(None, 'col'), may hold values from -6 to 6
- kernel: bfloat16 [3, 3, 3, 32, 40], replicated, may hold values from -0.1875 to 0.1875
- cotangent: bfloat16 [32, 48, 256, 128], P(None, 'disp', 'col'), may hold values from -14 to 14
Outputs:
- grad_left: bfloat16 [320, 256, 128], P('disp', 'col')
- grad_right: bfloat16 [320, 256, 128], P('disp', 'col')
- grad_kernel: float32 [3, 3, 3, 32, 40], replicated
The draws below stay inside these ranges and needn't reach their ends.
All inputs are finite; a program needn't handle non-finite values.
Results may differ from the reference program's by a relative error of at most 0.0034.
The reference program's roundings to bfloat16 on the way count: a program that leaves them out, or rounds other values in their place, can miss the bound.
Values may be sent and summed in bfloat16 or wider, within the bound.
A program may use at most 64 MiB of HBM per device.

```python
import math
import jax
import jax.numpy as jnp
from jax import lax

C = 320
G = 40
D = 48
O = 32
ROWS = 128
NX = 256


def draw_cotangent(key, part):
    first_key = jax.random.fold_in(jax.random.fold_in(key, 17), 0)
    column_ramp = 0.5 + 1.5 * jnp.arange(NX, dtype=jnp.float32) / max(NX - 1, 1)
    base_draw = jnp.clip(jax.random.normal(first_key, (O, D, NX, ROWS), jnp.float32), -4.0, 4.0)
    return (base_draw * column_ramp[None, None, :, None]).astype(jnp.bfloat16)


def steps_of(stream_key, extent, pieces, smallest, high):
    gain, own = 1.0, jax.random.fold_in(stream_key, 6)
    for axis_at, parts in pieces:
        steps = jnp.exp(jax.random.uniform(jax.random.fold_in(own, axis_at), (parts,), jnp.float32, smallest / len(pieces), high / len(pieces)))
        gain = gain * jnp.repeat(steps, extent[axis_at] // parts).reshape([-1 if axis == axis_at else 1 for axis in range(len(extent))])
    return gain


def centred(key, shape, scale, limit, pieces=(), kind=jnp.bfloat16):
    factor_of = steps_of(key, shape, pieces, -0.22, 0.18) if pieces else 1.0
    drawn = jax.random.normal(key, shape, jnp.float32) * scale * factor_of
    return jnp.minimum(jnp.maximum(drawn, -limit), limit).astype(kind)


def setup_inputs(seed: int = 0) -> dict:
    keys = jax.random.split(jax.random.key(seed), 5)
    left = centred(keys[0], (C, NX, ROWS), 1.0, 6.0, ((1, 32),))
    right = centred(keys[1], (C, NX, ROWS), 1.0, 6.0, ((1, 32),))
    kernel = centred(keys[2], (3, 3, 3, O, G), (27 * G) ** -0.5, 0.1875)
    cotangent = draw_cotangent(jax.random.fold_in(keys[4], 71), 0)
    return dict(left=left, right=right, kernel=kernel, cotangent=cotangent)


def shifted(feature, amount):
    columns = feature.shape[1]
    padded = jnp.pad(feature, ((0, 0), (D, 0), (0, 0)))
    return lax.dynamic_slice_in_dim(padded, (D - amount).astype(jnp.int32), columns, 1)

def volume_of(left, right, amount):
    channels, columns, row_count = left.shape
    group_size = C // G
    inside = ((amount >= 0) & (amount < D)).astype(jnp.float32)
    clipped = jnp.clip(amount, 0, D - 1).astype(jnp.int32)
    product = left.astype(jnp.float32) * shifted(right, clipped).astype(jnp.float32)
    volume = product.reshape(G, group_size, columns, row_count).sum(1) / group_size
    return (volume * inside).astype(jnp.bfloat16)

def reference(left, right, kernel, cotangent):
    channels, columns, row_count = left.shape
    group_size = C // G
    kernel_float = kernel.astype(jnp.float32)
    cotangent_pad = jnp.pad(cotangent, ((0, 0), (1, 1), (1, 1), (1, 1)))

    def advance(state_now, amount):
        kernel_grad, left_grad, right_grad = state_now
        cotangent_now = lax.dynamic_index_in_dim(cotangent, amount, 1, keepdims=False).astype(jnp.float32)
        updates = []
        for depth_tap in range(3):
            volume = volume_of(left, right, amount + depth_tap - 1)
            volume_pad = jnp.pad(volume, ((0, 0), (1, 1), (1, 1))).astype(jnp.float32)
            for column_tap in range(3):
                for row_tap in range(3):
                    window = volume_pad[:, column_tap:column_tap + columns, row_tap:row_tap + row_count]
                    updates.append(jnp.einsum('owh,gwh->og', cotangent_now, window))
        kernel_grad = kernel_grad + jnp.stack(updates, 0).reshape(3, 3, 3, O, G)
        grad_vol = jnp.zeros((G, columns, row_count), jnp.float32)
        for depth_tap in range(3):
            slab = lax.dynamic_index_in_dim(cotangent_pad, amount + 2 - depth_tap, 1, keepdims=False).astype(jnp.float32)
            for column_tap in range(3):
                for row_tap in range(3):
                    window = slab[:, 2 - column_tap:2 - column_tap + columns, 2 - row_tap:2 - row_tap + row_count]
                    grad_vol = grad_vol + jnp.einsum('og,owh->gwh', kernel_float[depth_tap, column_tap, row_tap], window)
        grad_vol = lax.optimization_barrier(grad_vol.astype(jnp.bfloat16)).astype(jnp.float32)
        spread = jnp.broadcast_to(grad_vol[:, None], (G, group_size, columns, row_count)).reshape(channels, columns, row_count)
        left_grad = left_grad + spread * shifted(right, amount).astype(jnp.float32)
        start = (D - amount).astype(jnp.int32)
        current = lax.dynamic_slice_in_dim(right_grad, start, columns, 1)
        right_grad = lax.dynamic_update_slice_in_dim(right_grad, current + spread * left.astype(jnp.float32), start, 1)
        return ((kernel_grad, left_grad, right_grad), None)
    initial = (jnp.zeros((3, 3, 3, O, G), jnp.float32), jnp.zeros((channels, columns, row_count), jnp.float32), jnp.zeros((channels, D + columns, row_count), jnp.float32))
    final, unused = lax.scan(advance, initial, jnp.arange(D, dtype=jnp.int32))
    kernel_grad, left_grad, right_grad = final
    grad_left = (left_grad / group_size).astype(jnp.bfloat16)
    grad_right = (right_grad[:, D:] / group_size).astype(jnp.bfloat16)
    grad_kernel = kernel_grad * (1.0 / math.sqrt(D * columns * row_count))
    return (grad_left, grad_right, grad_kernel)
```

```python
import math

import jax
import jax.numpy as jnp
from jax import lax
from jax.experimental import pallas as pl
from jax.experimental.pallas import tpu as pltpu
from jax.sharding import PartitionSpec as P

C = 320
G = 40
D = 48
O = 32
NCOL = 32
NY = 4
NZ = 8
ND = 8
DL = D // ND
CL = C // ND
GL = G // ND
GS = C // G
W = 8
H = 128
REACH = 6
K = 27 * O
F32 = jnp.float32
BF16 = jnp.bfloat16


def kernel(
    cot, wgt, left_hbm, right_hbm,
    gl_out, gr_out, ks_out,
    halo_w, halo_d, halo_c, e3, lb, rb, rx, lf,
    gvt, gvr, vot, vor, tmp, vtmp, grx, gsend, mrecv, precv,
    acc, ksp, kd, ky, kz, kf,
    local_sems, send_sems, recv_sems,
):
    c = lax.axis_index("col")
    k = lax.axis_index("disp")
    y = c // NZ
    z = c % NZ

    def at(dc=0, dk=0):
        return {"col": (c + dc + NCOL) % NCOL, "disp": (k + dk + ND) % ND}

    def zpeer(r):
        return {"col": y * NZ + (z + r) % NZ, "disp": k}

    def ypeer(r):
        return {"col": ((y + r) % NY) * NZ + z, "disp": k}

    barrier = pltpu.get_barrier_semaphore()
    peers = [at(0, r) for r in range(1, ND)]
    peers += [at(dc, dk) for dc in (-1, 1) for dk in (-1, 0, 1)]
    peers += [at(6, 0), at(-6, 0)]
    peers += [zpeer(r) for r in range(1, NZ)]
    peers += [ypeer(r) for r in range(1, NY)]
    for peer in peers:
        pl.semaphore_signal(barrier, inc=1, device_id=peer, device_id_type=pl.DeviceIdType.MESH)

    count = [0]
    pending = []

    def send(src, dst, peer):
        copy = pltpu.make_async_remote_copy(
            src_ref=src,
            dst_ref=dst,
            send_sem=send_sems.at[count[0]],
            recv_sem=recv_sems.at[count[0]],
            device_id=peer,
            device_id_type=pl.DeviceIdType.MESH,
        )
        count[0] += 1
        pending.append(copy)
        copy.start()
        return copy

    local_right = pltpu.make_async_copy(right_hbm.at[pl.ds(k * CL, CL)], rb.at[0], local_sems.at[0])
    local_left = pltpu.make_async_copy(left_hbm.at[pl.ds(k * CL, CL)], lb, local_sems.at[1])
    local_right.start()
    local_left.start()
    pl.semaphore_wait(barrier, len(peers))

    halos = [
        send(cot.at[:, W - 1], halo_w.at[0], at(1, 0)),
        send(cot.at[:, 0], halo_w.at[1], at(-1, 0)),
        send(cot.at[DL - 1], halo_d.at[0], at(0, 1)),
        send(cot.at[0], halo_d.at[1], at(0, -1)),
        send(cot.at[DL - 1, W - 1], halo_c.at[0], at(1, 1)),
        send(cot.at[DL - 1, 0], halo_c.at[1], at(-1, 1)),
        send(cot.at[0, W - 1], halo_c.at[2], at(1, -1)),
        send(cot.at[0, 0], halo_c.at[3], at(-1, -1)),
    ]
    local_right.wait()
    right_up = send(rb.at[0], rb.at[1], at(1, 0))
    right_down = send(rb.at[0], rb.at[6], at(6, 0))

    lane = lax.broadcasted_iota(jnp.int32, (O, H), 1)

    def spread(block, ok, d, w):
        value = block.astype(F32)
        if ok is not None:
            value = jnp.where(ok, value, 0.0)
        above = jnp.where(lane == H - 1, 0.0, pltpu.roll(value, H - 1, 1))
        below = jnp.where(lane == 0, 0.0, pltpu.roll(value, 1, 1))
        e3[d, w, 0:O] = above.astype(BF16)
        e3[d, w, O : 2 * O] = value.astype(BF16)
        e3[d, w, 2 * O : 3 * O] = below.astype(BF16)

    @pl.loop(0, DL)
    def _(d):
        for w in range(W):
            spread(cot[d, w], None, d + 1, w + 1)

    for copy in halos:
        copy.wait_recv()
    right_up.wait_recv()
    right_up2 = send(rb.at[1], rb.at[2], at(1, 0))
    right_down.wait_recv()
    right_down2 = send(rb.at[6], rb.at[5], at(-1, 0))

    has = {(0, 0): None}
    lo_c, hi_c, lo_k, hi_k = (c > 0, c < NCOL - 1, k > 0, k < ND - 1)

    @pl.loop(0, DL)
    def _(d):
        spread(halo_w[0, d], lo_c, d + 1, 0)
        spread(halo_w[1, d], hi_c, d + 1, W + 1)

    @pl.loop(0, W)
    def _(w):
        spread(halo_d[0, w], lo_k, 0, w + 1)
        spread(halo_d[1, w], hi_k, DL + 1, w + 1)

    spread(halo_c[0], lo_c & lo_k, 0, 0)
    spread(halo_c[1], hi_c & lo_k, 0, W + 1)
    spread(halo_c[2], lo_c & hi_k, DL + 1, 0)
    spread(halo_c[3], hi_c & hi_k, DL + 1, W + 1)

    def taps(d, w):
        return jnp.concatenate(
            [e3[d + 2 - p, w + 2 - q] for p in range(3) for q in range(3)], axis=0
        )

    @pl.loop(0, DL)
    def _(d):
        for w in range(0, W, 2):
            stack = jnp.concatenate([taps(d, w), taps(d, w + 1)], axis=1)
            out = jnp.dot(wgt[...], stack, preferred_element_type=F32)
            tmp[w * G : (w + 1) * G] = out[:, :H]
            tmp[(w + 1) * G : (w + 2) * G] = out[:, H:]
        for g in range(G):
            gvt[g // GL, g % GL, d] = tmp[pl.ds(g, W, stride=G)].astype(BF16)

    gv_copies = [
        send(gvt.at[(k + r) % ND], gvr.at[k], at(0, r)) for r in range(1, ND)
    ]
    gvr[k] = gvt[k]

    right_up2.wait_recv()
    right_up3 = send(rb.at[2], rb.at[3], at(1, 0))
    right_down2.wait_recv()
    right_down3 = send(rb.at[5], rb.at[4], at(-1, 0))
    local_left.wait()
    lf[...] = lb[...].astype(F32)
    right_up3.wait_recv()
    right_down3.wait_recv()
    for j in range(REACH + 1):
        block = rb[j].astype(F32)
        if j:
            block = jnp.where(c >= j, block, 0.0)
        rx[:, D - W * j : D - W * j + W] = block

    @pl.loop(0, GL)
    def _(g):
        for d in range(D):
            total = None
            for i in range(GS):
                term = lf[g * GS + i] * rx[g * GS + i, D - d : D - d + W]
                total = term if total is None else total + term
            vot[d // DL, g, d % DL] = (total * (1.0 / GS)).astype(BF16)

    vo_copies = [
        send(vot.at[(k + r) % ND], vor.at[k], at(0, r)) for r in range(1, ND)
    ]
    vor[k] = vot[k]

    for copy in gv_copies:
        copy.wait_recv()

    grx[...] = jnp.zeros_like(grx)

    @pl.loop(0, GL)
    def _(g):
        sums = [jnp.zeros((W, H), F32) for _ in range(GS)]
        for d in range(D):
            grad = gvr[d // DL, g, d % DL].astype(F32)
            for i in range(GS):
                ch = g * GS + i
                sums[i] = sums[i] + grad * rx[ch, D - d : D - d + W]
                grx[ch, D - d : D - d + W] += grad * lf[ch]
        for i in range(GS):
            gl_out[g * GS + i] = (sums[i] * (1.0 / GS)).astype(BF16)

    def own(j):
        return jnp.where(c >= j, grx[:, D - W * j : D - W * j + W], 0.0)

    gsend[3] = own(3)
    down1 = send(gsend.at[3], mrecv.at[0], at(-1, 0))
    gsend[4] = own(4)
    up1 = send(gsend.at[4], precv.at[0], at(1, 0))

    for copy in vo_copies:
        copy.wait_recv()
    acc[...] = jnp.zeros_like(acc)

    @pl.loop(0, DL)
    def _(d):
        for part in range(ND):
            for g in range(GL):
                vtmp[(part * GL + g) * W : (part * GL + g + 1) * W] = vor[part, g, d].astype(F32)
        for w in range(0, W, 2):
            vol = jnp.concatenate(
                [vtmp[pl.ds(w, G, stride=W)], vtmp[pl.ds(w + 1, G, stride=W)]], axis=1
            ).astype(BF16)
            stack = jnp.concatenate([taps(d, w), taps(d, w + 1)], axis=1)
            acc[:, :K] += lax.dot_general(
                vol, stack, (((1,), (1,)), ((), ())), preferred_element_type=F32
            )

    for part in range(ND):
        ksp[part] = acc[:, part * H : (part + 1) * H]
    kd_copies = [send(ksp.at[(k + r) % ND], kd.at[k], at(0, r)) for r in range(1, ND)]
    kd[k] = ksp[k]

    down1.wait_recv()
    gsend[2] = own(2) + mrecv[0]
    down2 = send(gsend.at[2], mrecv.at[1], at(-1, 0))
    up1.wait_recv()
    gsend[5] = own(5) + precv[0]
    up2 = send(gsend.at[5], precv.at[1], at(1, 0))

    def total_of(ref, count):
        value = ref[0]
        for i in range(1, count):
            value = value + ref[i]
        return value

    for copy in kd_copies:
        copy.wait_recv()
    ksp[ND] = total_of(kd, ND)
    ky[y] = ksp[ND]
    ky_copies = [send(ksp.at[ND], ky.at[y], ypeer(r)) for r in range(1, NY)]

    down2.wait_recv()
    gsend[1] = own(1) + mrecv[1]
    down3 = send(gsend.at[1], mrecv.at[2], at(-1, 0))
    up2.wait_recv()
    gsend[6] = own(6) + precv[1]
    up3 = send(gsend.at[6], precv.at[2], at(-6, 0))

    for copy in ky_copies:
        copy.wait_recv()
    ksp[ND + 1] = total_of(ky, NY)
    kz[z] = ksp[ND + 1]
    kz_copies = [send(ksp.at[ND + 1], kz.at[z], zpeer(r)) for r in range(1, NZ)]
    for copy in kz_copies:
        copy.wait_recv()
    ksp[ND + 2] = total_of(kz, NZ)
    kf[k] = ksp[ND + 2]
    kf_copies = [send(ksp.at[ND + 2], kf.at[k], at(0, r)) for r in range(1, ND)]

    down3.wait_recv()
    up3.wait_recv()
    total = grx[:, D : D + W] + mrecv[2] + precv[2]
    gr_out[...] = (total * (1.0 / GS)).astype(BF16)
    for copy in kf_copies:
        copy.wait_recv()
    ks_out[...] = kf[...]
    for copy in pending:
        copy.wait_send()


N_SENDS = 8 + 6 + 7 + 7 + 6 + 7 + 3 + 7 + 7


def body(left, right, kernel_weights, cotangent):
    cot = jnp.transpose(cotangent, (1, 2, 0, 3))
    wgt = kernel_weights.reshape(K, G).T
    vmem = pl.BlockSpec(memory_space=pltpu.VMEM)
    hbm = pl.BlockSpec(memory_space=pl.ANY)
    half = lambda *shape: pltpu.VMEM(shape, BF16)
    full = lambda *shape: pltpu.VMEM(shape, F32)
    left_out, right_out, parts = pl.pallas_call(
        kernel,
        out_shape=(
            jax.ShapeDtypeStruct((CL, W, H), BF16),
            jax.ShapeDtypeStruct((CL, W, H), BF16),
            jax.ShapeDtypeStruct((ND, G, H), F32),
        ),
        in_specs=[vmem, vmem, hbm, hbm],
        out_specs=(vmem, vmem, vmem),
        scratch_shapes=[
            half(2, DL, O, H),
            half(2, W, O, H),
            half(4, O, H),
            half(DL + 2, W + 2, 3 * O, H),
            half(CL, W, H),
            half(REACH + 1, CL, W, H),
            full(CL, D + W, H),
            full(CL, W, H),
            half(ND, GL, DL, W, H),
            half(ND, GL, DL, W, H),
            half(ND, GL, DL, W, H),
            half(ND, GL, DL, W, H),
            full(W * G, H),
            full(W * G, H),
            full(CL, D + W, H),
            full(REACH + 1, CL, W, H),
            full(3, CL, W, H),
            full(3, CL, W, H),
            full(G, ND * H),
            full(ND + 3, G, H),
            full(ND, G, H),
            full(NY, G, H),
            full(NZ, G, H),
            full(ND, G, H),
            pltpu.SemaphoreType.DMA((2,)),
            pltpu.SemaphoreType.DMA((N_SENDS,)),
            pltpu.SemaphoreType.DMA((N_SENDS,)),
        ],
        compiler_params=pltpu.CompilerParams(
            collective_id=0, has_side_effects=True, vmem_limit_bytes=48 * 1024 * 1024
        ),
    )(cot, wgt, left, right)
    sums = jnp.transpose(parts, (0, 2, 1)).reshape(ND * H, G)[:K]
    cells = D * NCOL * W * H
    grad_kernel = sums.reshape(3, 3, 3, O, G) * (1.0 / math.sqrt(cells))
    return (left_out, right_out, grad_kernel)


def solution(mesh):
    return jax.shard_map(
        body,
        mesh=mesh,
        in_specs=(P(None, "col", None), P(None, "col", None), P(), P(None, "disp", "col", None)),
        out_specs=(P("disp", "col", None), P("disp", "col", None), P()),
        check_vma=False,
    )
```

```python
import math

import jax
import jax.numpy as jnp
from jax import lax
from jax.experimental import pallas as pl
from jax.experimental.pallas import tpu as pltpu
from jax.sharding import PartitionSpec as P

C = 320
G = 40
D = 48
O = 32
NCOL = 32
NY = 4
NZ = 8
ND = 8
DL = D // ND
CL = C // ND
GL = G // ND
GS = C // G
W = 8
H = 128
REACH = 6
K = 27 * O
F32 = jnp.float32
BF16 = jnp.bfloat16


def kernel(
    cot, wgt, left_hbm, right_hbm,
    gl_out, gr_out, ks_out,
    halo_w, halo_d, halo_c, e3, lb, rb, rx, lf,
    gvt, gvr, vot, vor, tmp, vtmp, grx, gsend, mrecv, precv,
    acc, ksp, kd, ky, kz, kf,
    local_sems, send_sems, recv_sems,
):
    c = lax.axis_index("col")
    k = lax.axis_index("disp")
    y = c // NZ
    z = c % NZ

    def at(dc=0, dk=0):
        return {"col": (c + dc + NCOL) % NCOL, "disp": (k + dk + ND) % ND}

    def zpeer(r):
        return {"col": y * NZ + (z + r) % NZ, "disp": k}

    def ypeer(r):
        return {"col": ((y + r) % NY) * NZ + z, "disp": k}

    barrier = pltpu.get_barrier_semaphore()
    peers = [at(0, r) for r in range(1, ND)]
    peers += [at(dc, dk) for dc in (-1, 1) for dk in (-1, 0, 1)]
    peers += [at(6, 0), at(-6, 0)]
    peers += [zpeer(r) for r in range(1, NZ)]
    peers += [ypeer(r) for r in range(1, NY)]
    for peer in peers:
        pl.semaphore_signal(barrier, inc=1, device_id=peer, device_id_type=pl.DeviceIdType.MESH)

    def copy_of(src, dst, slot, peer):
        return pltpu.make_async_remote_copy(
            src_ref=src,
            dst_ref=dst,
            send_sem=send_sems.at[slot],
            recv_sem=recv_sems.at[slot],
            device_id=peer,
            device_id_type=pl.DeviceIdType.MESH,
        )

    def halo_copy(i):
        return (
            lambda: copy_of(cot.at[:, W - 1], halo_w.at[0], 0, at(1, 0)),
            lambda: copy_of(cot.at[:, 0], halo_w.at[1], 1, at(-1, 0)),
            lambda: copy_of(cot.at[DL - 1], halo_d.at[0], 2, at(0, 1)),
            lambda: copy_of(cot.at[0], halo_d.at[1], 3, at(0, -1)),
            lambda: copy_of(cot.at[DL - 1, W - 1], halo_c.at[0], 4, at(1, 1)),
            lambda: copy_of(cot.at[DL - 1, 0], halo_c.at[1], 5, at(-1, 1)),
            lambda: copy_of(cot.at[0, W - 1], halo_c.at[2], 6, at(1, -1)),
            lambda: copy_of(cot.at[0, 0], halo_c.at[3], 7, at(-1, -1)),
        )[i]()

    def right_copy(step, g):
        src, dst, hop = ((0, 1, 1), (1, 2, 1), (2, 3, 1), (0, 6, 6), (6, 5, -1), (5, 4, -1))[step]
        rows = pl.ds(g * GS, GS)
        return copy_of(rb.at[src, rows], rb.at[dst, rows], S_RIGHT + step * GL + g, at(hop, 0))

    def gv_copy(r, d):
        return copy_of(gvt.at[(k + r) % ND, d], gvr.at[k, d], S_GV + (r - 1) * DL + d, at(0, r))

    def vo_copy(r, g):
        return copy_of(vot.at[(k + r) % ND, g], vor.at[k, g], S_VO + (r - 1) * GL + g, at(0, r))

    def chain_copy(step, g):
        src, recv, slot, hop = (
            (3, mrecv, 0, -1), (2, mrecv, 1, -1), (1, mrecv, 2, -1),
            (4, precv, 0, 1), (5, precv, 1, 1), (6, precv, 2, -6),
        )[step]
        rows = pl.ds(g * GS, GS)
        return copy_of(
            gsend.at[src, rows], recv.at[slot, rows], S_CHAIN + step * GL + g, at(hop, 0)
        )

    def kd_copy(r):
        return copy_of(ksp.at[(k + r) % ND], kd.at[k], S_KD + r - 1, at(0, r))

    def ky_copy(r):
        return copy_of(ksp.at[ND], ky.at[y], S_KY + r - 1, ypeer(r))

    def kz_copy(r):
        return copy_of(ksp.at[ND + 1], kz.at[z], S_KZ + r - 1, zpeer(r))

    def kf_copy(r):
        return copy_of(ksp.at[ND + 2], kf.at[k], S_KF + r - 1, at(0, r))

    lane = lax.broadcasted_iota(jnp.int32, (O, H), 1)

    def spread(block, ok, d, w):
        value = block.astype(F32)
        if ok is not None:
            value = jnp.where(ok, value, 0.0)
        above = jnp.where(lane == H - 1, 0.0, pltpu.roll(value, H - 1, 1))
        below = jnp.where(lane == 0, 0.0, pltpu.roll(value, 1, 1))
        e3[d, w, 0:O] = above.astype(BF16)
        e3[d, w, O : 2 * O] = value.astype(BF16)
        e3[d, w, 2 * O : 3 * O] = below.astype(BF16)

    local_right = pltpu.make_async_copy(right_hbm.at[pl.ds(k * CL, CL)], rb.at[0], local_sems.at[0])
    local_left = pltpu.make_async_copy(left_hbm.at[pl.ds(k * CL, CL)], lb, local_sems.at[1])
    local_right.start()
    local_left.start()

    @pl.loop(0, DL)
    def _(d):
        for w in range(W):
            spread(cot[d, w], None, d + 1, w + 1)

    local_right.wait()
    pl.semaphore_wait(barrier, len(peers))
    for i in range(8):
        halo_copy(i).start()

    @pl.loop(0, GL)
    def _(g):
        right_copy(0, g).start()
        right_copy(3, g).start()

    local_left.wait()
    lf[...] = lb[...].astype(F32)

    @pl.loop(0, GL)
    def _(g):
        right_copy(0, g).wait_recv()
        right_copy(1, g).start()

    for i in range(8):
        halo_copy(i).wait_recv()
    lo_c, hi_c, lo_k, hi_k = (c > 0, c < NCOL - 1, k > 0, k < ND - 1)

    @pl.loop(0, DL)
    def _(d):
        spread(halo_w[0, d], lo_c, d + 1, 0)
        spread(halo_w[1, d], hi_c, d + 1, W + 1)

    @pl.loop(0, W)
    def _(w):
        spread(halo_d[0, w], lo_k, 0, w + 1)
        spread(halo_d[1, w], hi_k, DL + 1, w + 1)

    spread(halo_c[0], lo_c & lo_k, 0, 0)
    spread(halo_c[1], hi_c & lo_k, 0, W + 1)
    spread(halo_c[2], lo_c & hi_k, DL + 1, 0)
    spread(halo_c[3], hi_c & hi_k, DL + 1, W + 1)

    @pl.loop(0, GL)
    def _(g):
        right_copy(3, g).wait_recv()
        right_copy(4, g).start()

    def taps(d, w):
        return jnp.concatenate(
            [e3[d + 2 - p, w + 2 - q] for p in range(3) for q in range(3)], axis=0
        )

    @pl.loop(0, DL)
    def _(d):
        for w in range(0, W, 2):
            stack = jnp.concatenate([taps(d, w), taps(d, w + 1)], axis=1)
            out = jnp.dot(wgt[...], stack, preferred_element_type=F32)
            tmp[w * G : (w + 1) * G] = out[:, :H]
            tmp[(w + 1) * G : (w + 2) * G] = out[:, H:]
        for g in range(G):
            gvt[g // GL, d, g % GL] = tmp[pl.ds(g, W, stride=G)].astype(BF16)
        for r in range(1, ND):
            gv_copy(r, d).start()

        @pl.when(d < GL)
        def _():
            right_copy(1, d).wait_recv()
            right_copy(2, d).start()

    gvr[k] = gvt[k]

    @pl.loop(0, GL)
    def _(g):
        right_copy(4, g).wait_recv()
        right_copy(5, g).start()

    @pl.loop(0, GL)
    def _(g):
        right_copy(2, g).wait_recv()
        right_copy(5, g).wait_recv()
        rows = pl.ds(g * GS, GS)
        for j in range(REACH + 1):
            block = rb[j, rows].astype(F32)
            if j:
                block = jnp.where(c >= j, block, 0.0)
            rx[rows, D - W * j : D - W * j + W] = block
        for d in range(D):
            total = None
            for i in range(GS):
                term = lf[g * GS + i] * rx[g * GS + i, D - d : D - d + W]
                total = term if total is None else total + term
            vot[d // DL, g, d % DL] = (total * (1.0 / GS)).astype(BF16)
        for r in range(1, ND):
            vo_copy(r, g).start()

    vor[k] = vot[k]

    @pl.loop(0, DL)
    def _(d):
        for r in range(1, ND):
            gv_copy(r, d).wait_recv()

    def own(j, g):
        return jnp.where(c >= j, grx[pl.ds(g * GS, GS), D - W * j : D - W * j + W], 0.0)

    @pl.loop(0, GL)
    def _(g):
        rows = pl.ds(g * GS, GS)
        grx[rows] = jnp.zeros((GS, D + W, H), F32)
        sums = [jnp.zeros((W, H), F32) for _ in range(GS)]
        for d in range(D):
            grad = gvr[d // DL, d % DL, g].astype(F32)
            for i in range(GS):
                ch = g * GS + i
                sums[i] = sums[i] + grad * rx[ch, D - d : D - d + W]
                grx[ch, D - d : D - d + W] += grad * lf[ch]
        gsend[3, rows] = own(3, g)
        gsend[4, rows] = own(4, g)
        chain_copy(0, g).start()
        chain_copy(3, g).start()
        for i in range(GS):
            gl_out[g * GS + i] = (sums[i] * (1.0 / GS)).astype(BF16)

    @pl.loop(0, GL)
    def _(g):
        for r in range(1, ND):
            vo_copy(r, g).wait_recv()

    acc[...] = jnp.zeros_like(acc)

    @pl.loop(0, DL)
    def _(d):
        for part in range(ND):
            for g in range(GL):
                vtmp[(part * GL + g) * W : (part * GL + g + 1) * W] = vor[part, g, d].astype(F32)
        for w in range(0, W, 2):
            vol = jnp.concatenate(
                [vtmp[pl.ds(w, G, stride=W)], vtmp[pl.ds(w + 1, G, stride=W)]], axis=1
            ).astype(BF16)
            stack = jnp.concatenate([taps(d, w), taps(d, w + 1)], axis=1)
            acc[:, :K] += lax.dot_general(
                vol, stack, (((1,), (1,)), ((), ())), preferred_element_type=F32
            )

        @pl.when(d < GL)
        def _():
            rows = pl.ds(d * GS, GS)
            chain_copy(0, d).wait_recv()
            gsend[2, rows] = own(2, d) + mrecv[0, rows]
            chain_copy(1, d).start()
            chain_copy(3, d).wait_recv()
            gsend[5, rows] = own(5, d) + precv[0, rows]
            chain_copy(4, d).start()

    for part in range(ND):
        ksp[part] = acc[:, part * H : (part + 1) * H]
    for r in range(1, ND):
        kd_copy(r).start()
    kd[k] = ksp[k]

    @pl.loop(0, GL)
    def _(g):
        rows = pl.ds(g * GS, GS)
        chain_copy(4, g).wait_recv()
        gsend[6, rows] = own(6, g) + precv[1, rows]
        chain_copy(5, g).start()
        chain_copy(1, g).wait_recv()
        gsend[1, rows] = own(1, g) + mrecv[1, rows]
        chain_copy(2, g).start()

    def total_of(ref, count):
        value = ref[0]
        for i in range(1, count):
            value = value + ref[i]
        return value

    for r in range(1, ND):
        kd_copy(r).wait_recv()
    value = total_of(kd, ND)
    ksp[ND] = value
    ky[y] = value
    for r in range(1, NY):
        ky_copy(r).start()
    for r in range(1, NY):
        ky_copy(r).wait_recv()
    value = total_of(ky, NY)
    ksp[ND + 1] = value
    kz[z] = value
    for r in range(1, NZ):
        kz_copy(r).start()
    for r in range(1, NZ):
        kz_copy(r).wait_recv()
    value = total_of(kz, NZ)
    ksp[ND + 2] = value
    kf[k] = value
    for r in range(1, ND):
        kf_copy(r).start()

    @pl.loop(0, GL)
    def _(g):
        rows = pl.ds(g * GS, GS)
        chain_copy(2, g).wait_recv()
        chain_copy(5, g).wait_recv()
        total = grx[rows, D : D + W] + mrecv[2, rows] + precv[2, rows]
        gr_out[rows] = (total * (1.0 / GS)).astype(BF16)

    for r in range(1, ND):
        kf_copy(r).wait_recv()
    ks_out[...] = kf[...]

    for i in range(8):
        halo_copy(i).wait_send()

    @pl.loop(0, GL)
    def _(g):
        for step in range(6):
            right_copy(step, g).wait_send()
            chain_copy(step, g).wait_send()
        for r in range(1, ND):
            vo_copy(r, g).wait_send()

    @pl.loop(0, DL)
    def _(d):
        for r in range(1, ND):
            gv_copy(r, d).wait_send()

    for r in range(1, ND):
        kd_copy(r).wait_send()
        kz_copy(r).wait_send()
        kf_copy(r).wait_send()
    for r in range(1, NY):
        ky_copy(r).wait_send()


S_RIGHT = 8
S_GV = S_RIGHT + 6 * GL
S_VO = S_GV + (ND - 1) * DL
S_CHAIN = S_VO + (ND - 1) * GL
S_KD = S_CHAIN + 6 * GL
S_KY = S_KD + ND - 1
S_KZ = S_KY + NY - 1
S_KF = S_KZ + NZ - 1
N_SENDS = S_KF + ND - 1


def body(left, right, kernel_weights, cotangent):
    cot = jnp.transpose(cotangent, (1, 2, 0, 3))
    wgt = kernel_weights.reshape(K, G).T
    vmem = pl.BlockSpec(memory_space=pltpu.VMEM)
    hbm = pl.BlockSpec(memory_space=pltpu.HBM)
    half = lambda *shape: pltpu.VMEM(shape, BF16)
    full = lambda *shape: pltpu.VMEM(shape, F32)
    left_out, right_out, parts = pl.pallas_call(
        kernel,
        out_shape=(
            jax.ShapeDtypeStruct((CL, W, H), BF16),
            jax.ShapeDtypeStruct((CL, W, H), BF16),
            jax.ShapeDtypeStruct((ND, G, H), F32),
        ),
        in_specs=[vmem, vmem, hbm, hbm],
        out_specs=(vmem, vmem, vmem),
        scratch_shapes=[
            half(2, DL, O, H),
            half(2, W, O, H),
            half(4, O, H),
            half(DL + 2, W + 2, 3 * O, H),
            half(CL, W, H),
            half(REACH + 1, CL, W, H),
            full(CL, D + W, H),
            full(CL, W, H),
            half(ND, DL, GL, W, H),
            half(ND, DL, GL, W, H),
            half(ND, GL, DL, W, H),
            half(ND, GL, DL, W, H),
            full(W * G, H),
            full(W * G, H),
            full(CL, D + W, H),
            full(REACH + 1, CL, W, H),
            full(3, CL, W, H),
            full(3, CL, W, H),
            full(G, ND * H),
            full(ND + 3, G, H),
            full(ND, G, H),
            full(NY, G, H),
            full(NZ, G, H),
            full(ND, G, H),
            pltpu.SemaphoreType.DMA((2,)),
            pltpu.SemaphoreType.DMA((N_SENDS,)),
            pltpu.SemaphoreType.DMA((N_SENDS,)),
        ],
        compiler_params=pltpu.CompilerParams(
            collective_id=0, has_side_effects=True, vmem_limit_bytes=48 * 1024 * 1024
        ),
    )(cot, wgt, left, right)
    sums = jnp.transpose(parts, (0, 2, 1)).reshape(ND * H, G)[:K]
    cells = D * NCOL * W * H
    grad_kernel = sums.reshape(3, 3, 3, O, G) * (1.0 / math.sqrt(cells))
    return (left_out, right_out, grad_kernel)


def solution(mesh):
    return jax.shard_map(
        body,
        mesh=mesh,
        in_specs=(P(None, "col", None), P(None, "col", None), P(), P(None, "disp", "col", None)),
        out_specs=(P("disp", "col", None), P("disp", "col", None), P()),
        check_vma=False,
    )
```

```python
import math

import jax
import jax.numpy as jnp
from jax import lax
from jax.experimental import pallas as pl
from jax.experimental.pallas import tpu as pltpu
from jax.sharding import PartitionSpec as P

C = 320
G = 40
D = 48
O = 32
NCOL = 32
NY = 4
NZ = 8
ND = 8
DL = D // ND
CL = C // ND
GL = G // ND
GS = C // G
W = 8
H = 128
REACH = 6
K = 27 * O
F32 = jnp.float32
BF16 = jnp.bfloat16


def kernel(
    cot_hbm, wgt_hbm, left_hbm, right_hbm,
    gl_out, gr_out, ks_out,
    cotv, ctmp, wgt_in, wgt, halo_w, halo_d, halo_c, e3, lb, rb, rx, lf,
    gvt, gvr, vot, vor, tmp, vtmp, grx, gsend, mrecv, precv,
    acc, ksp, kd, ky, kz, kf,
    local_sems, send_sems, recv_sems,
):
    c = lax.axis_index("col")
    k = lax.axis_index("disp")
    y = c // NZ
    z = c % NZ

    def at(dc=0, dk=0):
        return {"col": (c + dc + NCOL) % NCOL, "disp": (k + dk + ND) % ND}

    def zpeer(r):
        return {"col": y * NZ + (z + r) % NZ, "disp": k}

    def ypeer(r):
        return {"col": ((y + r) % NY) * NZ + z, "disp": k}

    barrier = pltpu.get_barrier_semaphore()
    peers = [at(0, r) for r in range(1, ND)]
    peers += [at(dc, dk) for dc in (-1, 1) for dk in (-1, 0, 1)]
    peers += [at(6, 0), at(-6, 0)]
    peers += [zpeer(r) for r in range(1, NZ)]
    peers += [ypeer(r) for r in range(1, NY)]
    for peer in peers:
        pl.semaphore_signal(barrier, inc=1, device_id=peer, device_id_type=pl.DeviceIdType.MESH)

    def copy_of(src, dst, slot, peer):
        return pltpu.make_async_remote_copy(
            src_ref=src,
            dst_ref=dst,
            send_sem=send_sems.at[slot],
            recv_sem=recv_sems.at[slot],
            device_id=peer,
            device_id_type=pl.DeviceIdType.MESH,
        )

    ALL = pl.ds(1, DL)
    COLS = pl.ds(1, W)

    def own_rows(d, w):
        return e3.at[d, w, pl.ds(O, O)]

    def halo_copy(i):
        return (
            lambda: copy_of(own_rows(ALL, W), halo_w.at[0], 0, at(1, 0)),
            lambda: copy_of(own_rows(ALL, 1), halo_w.at[1], 1, at(-1, 0)),
            lambda: copy_of(own_rows(DL, COLS), halo_d.at[0], 2, at(0, 1)),
            lambda: copy_of(own_rows(1, COLS), halo_d.at[1], 3, at(0, -1)),
            lambda: copy_of(own_rows(DL, W), halo_c.at[0], 4, at(1, 1)),
            lambda: copy_of(own_rows(DL, 1), halo_c.at[1], 5, at(-1, 1)),
            lambda: copy_of(own_rows(1, W), halo_c.at[2], 6, at(1, -1)),
            lambda: copy_of(own_rows(1, 1), halo_c.at[3], 7, at(-1, -1)),
        )[i]()

    def right_copy(step, g):
        src, dst, hop = ((0, 1, 1), (1, 2, 1), (2, 3, 1), (0, 6, 6), (6, 5, -1), (5, 4, -1))[step]
        rows = pl.ds(g * GS, GS)
        return copy_of(rb.at[src, rows], rb.at[dst, rows], S_RIGHT + step * GL + g, at(hop, 0))

    def gv_copy(r, d):
        return copy_of(gvt.at[(k + r) % ND, d], gvr.at[k, d], S_GV + (r - 1) * DL + d, at(0, r))

    def vo_copy(r, d):
        return copy_of(vot.at[(k + r) % ND, d], vor.at[k, d], S_VO + (r - 1) * DL + d, at(0, r))

    def chain_copy(step, g):
        src, recv, slot, hop = (
            (3, mrecv, 0, -1), (2, mrecv, 1, -1), (1, mrecv, 2, -1),
            (4, precv, 0, 1), (5, precv, 1, 1), (6, precv, 2, -6),
        )[step]
        rows = pl.ds(g * GS, GS)
        return copy_of(
            gsend.at[src, rows], recv.at[slot, rows], S_CHAIN + step * GL + g, at(hop, 0)
        )

    def kd_copy(r):
        return copy_of(ksp.at[(k + r) % ND], kd.at[k], S_KD + r - 1, at(0, r))

    def ky_copy(r):
        return copy_of(ksp.at[ND], ky.at[y], S_KY + r - 1, ypeer(r))

    def kz_copy(r):
        return copy_of(ksp.at[ND + 1], kz.at[z], S_KZ + r - 1, zpeer(r))

    def kf_copy(r):
        return copy_of(ksp.at[ND + 2], kf.at[k], S_KF + r - 1, at(0, r))

    lane = lax.broadcasted_iota(jnp.int32, (O, H), 1)

    def spread(value, d, w):
        above = jnp.where(lane == H - 1, 0.0, pltpu.roll(value, H - 1, 1))
        below = jnp.where(lane == 0, 0.0, pltpu.roll(value, 1, 1))
        e3[d, w, 0:O] = above.astype(BF16)
        e3[d, w, O : 2 * O] = value.astype(BF16)
        e3[d, w, 2 * O : 3 * O] = below.astype(BF16)

    local_cot = pltpu.make_async_copy(cot_hbm, cotv, local_sems.at[2])
    local_right = pltpu.make_async_copy(right_hbm.at[pl.ds(k * CL, CL)], rb.at[0], local_sems.at[0])
    local_left = pltpu.make_async_copy(left_hbm.at[pl.ds(k * CL, CL)], lb, local_sems.at[1])
    local_wgt = pltpu.make_async_copy(wgt_hbm, wgt_in, local_sems.at[3])
    local_cot.start()
    local_wgt.start()
    local_right.start()
    local_left.start()
    local_cot.wait()

    @pl.loop(0, DL)
    def _(d):
        for o in range(O):
            ctmp[o * W : (o + 1) * W] = cotv[o, d].astype(F32)
        for w in range(W):
            spread(ctmp[pl.ds(w, O, stride=W)], d + 1, w + 1)

    eye = (
        lax.broadcasted_iota(jnp.int32, (G, G), 0) == lax.broadcasted_iota(jnp.int32, (G, G), 1)
    ).astype(F32)
    local_wgt.wait()
    wgt[...] = lax.dot_general(
        eye.astype(BF16), wgt_in[...], (((1,), (1,)), ((), ())), preferred_element_type=F32
    ).astype(BF16)
    local_left.wait()
    lf[...] = lb[...].astype(F32)
    local_right.wait()
    pl.semaphore_wait(barrier, len(peers))
    for i in range(8):
        halo_copy(i).start()

    @pl.loop(0, GL)
    def _(g):
        right_copy(3, g).start()
        right_copy(0, g).start()

    lo_c, hi_c, lo_k, hi_k = (c > 0, c < NCOL - 1, k > 0, k < ND - 1)

    def border(block, ok, d, w):
        spread(jnp.where(ok, block.astype(F32), 0.0), d, w)

    for i in range(2, 4):
        halo_copy(i).wait_recv()

    @pl.loop(0, W)
    def _(w):
        border(halo_d[0, w], lo_k, 0, w + 1)
        border(halo_d[1, w], hi_k, DL + 1, w + 1)

    for i in range(2):
        halo_copy(i).wait_recv()

    @pl.loop(0, DL)
    def _(d):
        border(halo_w[0, d], lo_c, d + 1, 0)
        border(halo_w[1, d], hi_c, d + 1, W + 1)

    for i in range(4, 8):
        halo_copy(i).wait_recv()
    border(halo_c[0], lo_c & lo_k, 0, 0)
    border(halo_c[1], hi_c & lo_k, 0, W + 1)
    border(halo_c[2], lo_c & hi_k, DL + 1, 0)
    border(halo_c[3], hi_c & hi_k, DL + 1, W + 1)

    def hand_on(step):
        @pl.loop(0, GL)
        def _(g):
            right_copy(step, g).wait_recv()
            right_copy(step + 1, g).start()

    hand_on(0)

    def taps(d, w):
        return jnp.concatenate(
            [e3[d + 2 - p, w + 2 - q] for p in range(3) for q in range(3)], axis=0
        )

    def grad_volume(first, last):
        @pl.loop(first, last)
        def _(d):
            for w in range(0, W, 2):
                stack = jnp.concatenate([taps(d, w), taps(d, w + 1)], axis=1)
                out = jnp.dot(wgt[...], stack, preferred_element_type=F32)
                tmp[w * G : (w + 1) * G] = out[:, :H]
                tmp[(w + 1) * G : (w + 2) * G] = out[:, H:]
            for g in range(G):
                gvt[g // GL, d, g % GL] = tmp[pl.ds(g, W, stride=G)].astype(BF16)
            for r in range(1, ND):
                gv_copy(r, d).start()

    grad_volume(0, 1)
    hand_on(3)
    grad_volume(1, 2)
    hand_on(1)
    grad_volume(2, 3)
    hand_on(4)
    grad_volume(3, DL)
    gvr[k] = gvt[k]

    @pl.loop(0, GL)
    def _(g):
        right_copy(2, g).wait_recv()
        rows = pl.ds(g * GS, GS)
        for j in (0, 1, 2, 3, 5, 6):
            block = rb[j, rows].astype(F32)
            if j:
                block = jnp.where(c >= j, block, 0.0)
            rx[rows, D - W * j : D - W * j + W] = block
        right_copy(5, g).wait_recv()
        rx[rows, D - W * 4 : D - W * 3] = jnp.where(c >= 4, rb[4, rows].astype(F32), 0.0)

    for level in range(DL):

        @pl.loop(0, GL)
        def _(g):
            for part in range(ND):
                d = part * DL + level
                total = None
                for i in range(GS):
                    term = lf[g * GS + i] * rx[g * GS + i, D - d : D - d + W]
                    total = term if total is None else total + term
                vot[part, level, g] = (total * (1.0 / GS)).astype(BF16)

        for r in range(1, ND):
            vo_copy(r, level).start()

    vor[k] = vot[k]

    @pl.loop(0, DL)
    def _(d):
        for r in range(1, ND):
            gv_copy(r, d).wait_recv()

    def own(j, g):
        return jnp.where(c >= j, grx[pl.ds(g * GS, GS), D - W * j : D - W * j + W], 0.0)

    @pl.loop(0, GL)
    def _(g):
        rows = pl.ds(g * GS, GS)
        grx[rows] = jnp.zeros((GS, D + W, H), F32)
        sums = [jnp.zeros((W, H), F32) for _ in range(GS)]
        for d in range(D):
            grad = gvr[d // DL, d % DL, g].astype(F32)
            for i in range(GS):
                ch = g * GS + i
                sums[i] = sums[i] + grad * rx[ch, D - d : D - d + W]
                grx[ch, D - d : D - d + W] += grad * lf[ch]
        gsend[3, rows] = own(3, g)
        gsend[4, rows] = own(4, g)
        chain_copy(0, g).start()
        chain_copy(3, g).start()
        for i in range(GS):
            gl_out[g * GS + i] = (sums[i] * (1.0 / GS)).astype(BF16)

    acc[...] = jnp.zeros_like(acc)

    @pl.loop(0, DL)
    def _(d):
        for r in range(1, ND):
            vo_copy(r, d).wait_recv()
        for part in range(ND):
            for g in range(GL):
                vtmp[(part * GL + g) * W : (part * GL + g + 1) * W] = vor[part, d, g].astype(F32)
        for w in range(0, W, 2):
            vol = jnp.concatenate(
                [vtmp[pl.ds(w, G, stride=W)], vtmp[pl.ds(w + 1, G, stride=W)]], axis=1
            ).astype(BF16)
            stack = jnp.concatenate([taps(d, w), taps(d, w + 1)], axis=1)
            acc[:, :K] += lax.dot_general(
                vol, stack, (((1,), (1,)), ((), ())), preferred_element_type=F32
            )

        @pl.when(d < GL)
        def _():
            part = d
            rows = pl.ds(part * GS, GS)
            chain_copy(0, part).wait_recv()
            gsend[2, rows] = own(2, part) + mrecv[0, rows]
            chain_copy(1, part).start()
            chain_copy(3, part).wait_recv()
            gsend[5, rows] = own(5, part) + precv[0, rows]
            chain_copy(4, part).start()

    for part in range(ND):
        ksp[part] = acc[:, part * H : (part + 1) * H]
    for r in range(1, ND):
        kd_copy(r).start()
    kd[k] = ksp[k]

    @pl.loop(0, GL)
    def _(g):
        rows = pl.ds(g * GS, GS)
        chain_copy(4, g).wait_recv()
        gsend[6, rows] = own(6, g) + precv[1, rows]
        chain_copy(5, g).start()
        chain_copy(1, g).wait_recv()
        gsend[1, rows] = own(1, g) + mrecv[1, rows]
        chain_copy(2, g).start()

    def total_of(ref, count):
        value = ref[0]
        for i in range(1, count):
            value = value + ref[i]
        return value

    for r in range(1, ND):
        kd_copy(r).wait_recv()
    value = total_of(kd, ND)
    ksp[ND] = value
    ky[y] = value
    for r in range(1, NY):
        ky_copy(r).start()
    for r in range(1, NY):
        ky_copy(r).wait_recv()
    value = total_of(ky, NY)
    ksp[ND + 1] = value
    kz[z] = value
    for r in range(1, NZ):
        kz_copy(r).start()
    for r in range(1, NZ):
        kz_copy(r).wait_recv()
    value = total_of(kz, NZ)
    ksp[ND + 2] = value
    kf[k] = value
    for r in range(1, ND):
        kf_copy(r).start()

    @pl.loop(0, GL)
    def _(g):
        rows = pl.ds(g * GS, GS)
        chain_copy(2, g).wait_recv()
        chain_copy(5, g).wait_recv()
        total = grx[rows, D : D + W] + mrecv[2, rows] + precv[2, rows]
        gr_out[rows] = (total * (1.0 / GS)).astype(BF16)

    for r in range(1, ND):
        kf_copy(r).wait_recv()
    ks_out[...] = kf[...]

    for i in range(8):
        halo_copy(i).wait_send()

    @pl.loop(0, GL)
    def _(g):
        for step in range(6):
            right_copy(step, g).wait_send()
            chain_copy(step, g).wait_send()

    @pl.loop(0, DL)
    def _(d):
        for r in range(1, ND):
            gv_copy(r, d).wait_send()
            vo_copy(r, d).wait_send()

    for r in range(1, ND):
        kd_copy(r).wait_send()
        kz_copy(r).wait_send()
        kf_copy(r).wait_send()
    for r in range(1, NY):
        ky_copy(r).wait_send()


S_RIGHT = 8
S_GV = S_RIGHT + 6 * GL
S_VO = S_GV + (ND - 1) * DL
S_CHAIN = S_VO + (ND - 1) * DL
S_KD = S_CHAIN + 6 * GL
S_KY = S_KD + ND - 1
S_KZ = S_KY + NY - 1
S_KF = S_KZ + NZ - 1
N_SENDS = S_KF + ND - 1


def finish(gl_in, gr_in, ks_in, gl_out, gr_out, ks_out, ksv, sems):
    copies = [
        pltpu.make_async_copy(gl_in, gl_out, sems.at[0]),
        pltpu.make_async_copy(gr_in, gr_out, sems.at[1]),
    ]
    for copy in copies:
        copy.start()
    cells = D * NCOL * W * H
    for part in range(ND):
        rows = min(H, K - part * H)
        if rows <= 0:
            break
        square = jnp.concatenate([ks_in[part], jnp.zeros((H - G, H), F32)], axis=0)
        flipped = jnp.transpose(square) * (1.0 / math.sqrt(cells))
        ksv[part * H : part * H + rows] = flipped[:rows, :G]
    last = pltpu.make_async_copy(ksv, ks_out, sems.at[2])
    last.start()
    for copy in copies + [last]:
        copy.wait()


def body(left, right, kernel_weights, cotangent):
    weights = kernel_weights.reshape(K, G)
    vmem = pl.BlockSpec(memory_space=pltpu.VMEM)
    hbm = pl.BlockSpec(memory_space=pltpu.HBM)
    half = lambda *shape: pltpu.VMEM(shape, BF16)
    full = lambda *shape: pltpu.VMEM(shape, F32)
    left_grad, right_grad, parts = pl.pallas_call(
        kernel,
        out_shape=(
            jax.ShapeDtypeStruct((CL, W, H), BF16),
            jax.ShapeDtypeStruct((CL, W, H), BF16),
            jax.ShapeDtypeStruct((ND, G, H), F32),
        ),
        in_specs=[hbm, hbm, hbm, hbm],
        out_specs=(vmem, vmem, vmem),
        scratch_shapes=[
            half(O, DL, W, H),
            full(O * W, H),
            half(K, G),
            half(G, K),
            half(2, DL, O, H),
            half(2, W, O, H),
            half(4, O, H),
            half(DL + 2, W + 2, 3 * O, H),
            half(CL, W, H),
            half(REACH + 1, CL, W, H),
            full(CL, D + W, H),
            full(CL, W, H),
            half(ND, DL, GL, W, H),
            half(ND, DL, GL, W, H),
            half(ND, DL, GL, W, H),
            half(ND, DL, GL, W, H),
            full(W * G, H),
            full(W * G, H),
            full(CL, D + W, H),
            full(REACH + 1, CL, W, H),
            full(3, CL, W, H),
            full(3, CL, W, H),
            full(G, ND * H),
            full(ND + 3, G, H),
            full(ND, G, H),
            full(NY, G, H),
            full(NZ, G, H),
            full(ND, G, H),
            pltpu.SemaphoreType.DMA((4,)),
            pltpu.SemaphoreType.DMA((N_SENDS,)),
            pltpu.SemaphoreType.DMA((N_SENDS,)),
        ],
        compiler_params=pltpu.CompilerParams(
            collective_id=0, has_side_effects=True, vmem_limit_bytes=48 * 1024 * 1024
        ),
    )(*[pltpu.with_memory_space_constraint(a, pltpu.HBM) for a in (cotangent, weights, left, right)])
    left_out, right_out, sums = pl.pallas_call(
        finish,
        out_shape=(
            jax.ShapeDtypeStruct((CL, W, H), BF16),
            jax.ShapeDtypeStruct((CL, W, H), BF16),
            jax.ShapeDtypeStruct((K, G), F32),
        ),
        in_specs=[vmem, vmem, vmem],
        out_specs=(hbm, hbm, hbm),
        scratch_shapes=[full(K, G), pltpu.SemaphoreType.DMA((3,))],
        compiler_params=pltpu.CompilerParams(vmem_limit_bytes=48 * 1024 * 1024),
    )(left_grad, right_grad, parts)
    return (left_out, right_out, sums.reshape(3, 3, 3, O, G))


def solution(mesh):
    return jax.shard_map(
        body,
        mesh=mesh,
        in_specs=(P(None, "col", None), P(None, "col", None), P(), P(None, "disp", "col", None)),
        out_specs=(P("disp", "col", None), P("disp", "col", None), P()),
        check_vma=False,
    )
```

```python
import math

import jax
import jax.numpy as jnp
from jax import lax
from jax.experimental import pallas as pl
from jax.experimental.pallas import tpu as pltpu
from jax.sharding import PartitionSpec as P

C = 320
G = 40
D = 48
O = 32
NCOL = 32
NY = 4
NZ = 8
ND = 8
DL = D // ND
CL = C // ND
GL = G // ND
GS = C // G
W = 8
H = 128
REACH = 6
K = 27 * O
F32 = jnp.float32
BF16 = jnp.bfloat16


def kernel(
    cot_hbm, wgt_hbm, left_hbm, right_hbm,
    gl_out, gr_out, ks_out,
    cotv, ctmp, wgt_in, wgt, halo_w, halo_d, halo_c, e3, lb, rb, rx, lf,
    gvt, gvr, vot, vor, tmp, vtmp, grx, gsend, mrecv, precv,
    acc, ksp, kd, ky, kz, kf,
    local_sems, send_sems, recv_sems,
):
    c = lax.axis_index("col")
    k = lax.axis_index("disp")
    y = c // NZ
    z = c % NZ

    def at(dc=0, dk=0):
        return {"col": (c + dc + NCOL) % NCOL, "disp": (k + dk + ND) % ND}

    def zpeer(r):
        return {"col": y * NZ + (z + r) % NZ, "disp": k}

    def ypeer(r):
        return {"col": ((y + r) % NY) * NZ + z, "disp": k}

    barrier = pltpu.get_barrier_semaphore()
    peers = [at(0, r) for r in range(1, ND)]
    peers += [at(dc, dk) for dc in (-1, 1) for dk in (-1, 0, 1)]
    peers += [at(6, 0), at(-6, 0)]
    peers += [zpeer(r) for r in range(1, NZ)]
    peers += [ypeer(r) for r in range(1, NY)]
    for peer in peers:
        pl.semaphore_signal(barrier, inc=1, device_id=peer, device_id_type=pl.DeviceIdType.MESH)

    def copy_of(src, dst, slot, peer, recv_slot=None):
        return pltpu.make_async_remote_copy(
            src_ref=src,
            dst_ref=dst,
            send_sem=send_sems.at[slot],
            recv_sem=recv_sems.at[slot if recv_slot is None else recv_slot],
            device_id=peer,
            device_id_type=pl.DeviceIdType.MESH,
        )

    ALL = pl.ds(1, DL)
    COLS = pl.ds(1, W)

    def own_rows(d, w):
        return e3.at[d, w, pl.ds(O, O)]

    def halo_copy(i):
        return (
            lambda: copy_of(own_rows(ALL, W), halo_w.at[0], 0, at(1, 0)),
            lambda: copy_of(own_rows(ALL, 1), halo_w.at[1], 1, at(-1, 0)),
            lambda: copy_of(own_rows(DL, COLS), halo_d.at[0], 2, at(0, 1)),
            lambda: copy_of(own_rows(1, COLS), halo_d.at[1], 3, at(0, -1)),
            lambda: copy_of(own_rows(DL, W), halo_c.at[0], 4, at(1, 1)),
            lambda: copy_of(own_rows(DL, 1), halo_c.at[1], 5, at(-1, 1)),
            lambda: copy_of(own_rows(1, W), halo_c.at[2], 6, at(1, -1)),
            lambda: copy_of(own_rows(1, 1), halo_c.at[3], 7, at(-1, -1)),
        )[i]()

    def right_copy(step, g):
        src, dst, hop = ((0, 1, 1), (1, 2, 1), (2, 3, 1), (0, 6, 6), (6, 5, -1), (5, 4, -1))[step]
        rows = pl.ds(g * GS, GS)
        source = rb.at[src, rows] if src else right_hbm.at[pl.ds(k * CL + g * GS, GS)]
        return copy_of(source, rb.at[dst, rows], S_RIGHT + step * GL + g, at(hop, 0))

    def gv_copy(r, d):
        return copy_of(gvt.at[(k + r) % ND, d], gvr.at[k, d], S_GV + (r - 1) * DL + d, at(0, r))

    def vo_copy(part, d):
        return copy_of(
            vot.at[part, d], vor.at[k, d], S_VO + part * DL + d, at_disp(part), S_VO + k * DL + d
        )

    def vo_arrival(part, d):
        return copy_of(
            vot.at[part, d], vor.at[part, d], S_VO + part * DL + d, at_disp(part)
        )

    def at_disp(part):
        return {"col": c, "disp": part}

    def others(part, act):
        @pl.when(k != part)
        def _():
            act()

    def chain_copy(step, g):
        src, recv, slot, hop = (
            (3, mrecv, 0, -1), (2, mrecv, 1, -1), (1, mrecv, 2, -1),
            (4, precv, 0, 1), (5, precv, 1, 1), (6, precv, 2, -6),
        )[step]
        rows = pl.ds(g * GS, GS)
        return copy_of(
            gsend.at[src, rows], recv.at[slot, rows], S_CHAIN + step * GL + g, at(hop, 0)
        )

    def kd_copy(r):
        return copy_of(ksp.at[(k + r) % ND], kd.at[k], S_KD + r - 1, at(0, r))

    def ky_copy(r):
        return copy_of(ksp.at[ND], ky.at[y], S_KY + r - 1, ypeer(r))

    def kz_copy(r):
        return copy_of(ksp.at[ND + 1], kz.at[z], S_KZ + r - 1, zpeer(r))

    def kf_copy(r):
        return copy_of(ksp.at[ND + 2], kf.at[k], S_KF + r - 1, at(0, r))

    lane = lax.broadcasted_iota(jnp.int32, (O, H), 1)

    def spread(value, d, w):
        above = jnp.where(lane == H - 1, 0.0, pltpu.roll(value, H - 1, 1))
        below = jnp.where(lane == 0, 0.0, pltpu.roll(value, 1, 1))
        e3[d, w, 0:O] = above.astype(BF16)
        e3[d, w, O : 2 * O] = value.astype(BF16)
        e3[d, w, 2 * O : 3 * O] = below.astype(BF16)

    local_cot = pltpu.make_async_copy(cot_hbm, cotv, local_sems.at[2])
    local_right = pltpu.make_async_copy(right_hbm.at[pl.ds(k * CL, CL)], rb.at[0], local_sems.at[0])
    local_left = pltpu.make_async_copy(left_hbm.at[pl.ds(k * CL, CL)], lb, local_sems.at[1])
    local_wgt = pltpu.make_async_copy(wgt_hbm, wgt_in, local_sems.at[3])
    local_cot.start()
    local_wgt.start()
    local_right.start()
    local_left.start()
    local_cot.wait()

    @pl.loop(0, DL)
    def _(d):
        for o in range(O):
            ctmp[o * W : (o + 1) * W] = cotv[o, d].astype(F32)
        for w in range(W):
            spread(ctmp[pl.ds(w, O, stride=W)], d + 1, w + 1)

    pl.semaphore_wait(barrier, len(peers))
    for i in range(8):
        halo_copy(i).start()

    @pl.loop(0, GL)
    def _(g):
        right_copy(3, g).start()
        right_copy(0, g).start()

    eye = (
        lax.broadcasted_iota(jnp.int32, (G, G), 0) == lax.broadcasted_iota(jnp.int32, (G, G), 1)
    ).astype(F32)
    local_wgt.wait()
    wgt[...] = lax.dot_general(
        eye.astype(BF16), wgt_in[...], (((1,), (1,)), ((), ())), preferred_element_type=F32
    ).astype(BF16)
    local_left.wait()
    lf[...] = lb[...].astype(F32)
    local_right.wait()

    def hand_on(step, first=0, last=GL):
        @pl.loop(first, last)
        def _(g):
            right_copy(step, g).wait_recv()
            right_copy(step + 1, g).start()

    def taps(d, w):
        return jnp.concatenate(
            [e3[d + 2 - p, w + 2 - q] for p in range(3) for q in range(3)], axis=0
        )

    def products(first, last, pairs):
        @pl.loop(first, last)
        def _(d):
            for a, b in pairs:
                stack = jnp.concatenate([taps(d, a), taps(d, b)], axis=1)
                out = jnp.dot(wgt[...], stack, preferred_element_type=F32)
                tmp[d, a * G : (a + 1) * G] = out[:, :H]
                tmp[d, b * G : (b + 1) * G] = out[:, H:]

    def finish_levels(first, last):
        products(first, last, ((0, W - 1),))

        @pl.loop(first, last)
        def _(d):
            for g in range(G):
                gvt[g // GL, d, g % GL] = tmp[d, pl.ds(g, W, stride=G)].astype(BF16)
            for r in range(1, ND):
                gv_copy(r, d).start()

    inner = ((1, 2), (3, 4), (5, 6))
    products(1, DL - 1, inner)

    lo_c, hi_c, lo_k, hi_k = (c > 0, c < NCOL - 1, k > 0, k < ND - 1)

    def border(block, ok, d, w):
        spread(jnp.where(ok, block.astype(F32), 0.0), d, w)

    for i in range(2, 4):
        halo_copy(i).wait_recv()

    @pl.loop(0, W)
    def _(w):
        border(halo_d[0, w], lo_k, 0, w + 1)
        border(halo_d[1, w], hi_k, DL + 1, w + 1)

    hand_on(0, 0, 3)
    products(0, 1, inner)
    products(DL - 1, DL, inner)
    hand_on(0, 3)
    for i in range(2):
        halo_copy(i).wait_recv()

    @pl.loop(0, DL)
    def _(d):
        border(halo_w[0, d], lo_c, d + 1, 0)
        border(halo_w[1, d], hi_c, d + 1, W + 1)

    for i in range(4, 8):
        halo_copy(i).wait_recv()
    border(halo_c[0], lo_c & lo_k, 0, 0)
    border(halo_c[1], hi_c & lo_k, 0, W + 1)
    border(halo_c[2], lo_c & hi_k, DL + 1, 0)
    border(halo_c[3], hi_c & hi_k, DL + 1, W + 1)

    hand_on(3)
    finish_levels(0, 3)
    hand_on(1)
    finish_levels(3, DL)
    hand_on(4)
    gvr[k] = gvt[k]

    def widen(g, blocks):
        rows = pl.ds(g * GS, GS)
        for j in blocks:
            block = rb[j, rows].astype(F32)
            if j:
                block = jnp.where(c >= j, block, 0.0)
            rx[rows, D - W * j : D - W * j + W] = block

    def volume(parts):
        for level in range(DL):

            @pl.loop(0, GL)
            def _(g):
                for part in parts:
                    d = part * DL + level
                    total = None
                    for i in range(GS):
                        term = lf[g * GS + i] * rx[g * GS + i, D - d : D - d + W]
                        total = term if total is None else total + term
                    vot[part, level, g] = (total * (1.0 / GS)).astype(BF16)

            for part in parts:
                others(part, lambda: vo_copy(part, level).start())

    @pl.loop(0, GL)
    def _(g):
        right_copy(2, g).wait_recv()
        widen(g, (0, 1, 2, 3))

    volume((0, 1, 2, 3))

    @pl.loop(0, GL)
    def _(g):
        right_copy(5, g).wait_recv()
        widen(g, (4, 5, 6))

    volume((4, 5, 6, 7))
    vor[k] = vot[k]

    @pl.loop(0, DL)
    def _(d):
        for r in range(1, ND):
            gv_copy(r, d).wait_recv()

    def own(j, g):
        return jnp.where(c >= j, grx[pl.ds(g * GS, GS), D - W * j : D - W * j + W], 0.0)

    @pl.loop(0, GL)
    def _(g):
        rows = pl.ds(g * GS, GS)
        grx[rows] = jnp.zeros((GS, D + W, H), F32)
        sums = [jnp.zeros((W, H), F32) for _ in range(GS)]
        for d in range(D):
            grad = gvr[d // DL, d % DL, g].astype(F32)
            for i in range(GS):
                ch = g * GS + i
                sums[i] = sums[i] + grad * rx[ch, D - d : D - d + W]
                grx[ch, D - d : D - d + W] += grad * lf[ch]
        gsend[3, rows] = own(3, g)
        gsend[4, rows] = own(4, g)
        chain_copy(0, g).start()
        chain_copy(3, g).start()
        for i in range(GS):
            gl_out[g * GS + i] = (sums[i] * (1.0 / GS)).astype(BF16)

    acc[...] = jnp.zeros_like(acc)

    @pl.loop(0, DL)
    def _(d):
        for part in range(ND):
            others(part, lambda: vo_arrival(part, d).wait_recv())
        for part in range(ND):
            for g in range(GL):
                vtmp[(part * GL + g) * W : (part * GL + g + 1) * W] = vor[part, d, g].astype(F32)
        for w in range(0, W, 2):
            vol = jnp.concatenate(
                [vtmp[pl.ds(w, G, stride=W)], vtmp[pl.ds(w + 1, G, stride=W)]], axis=1
            ).astype(BF16)
            stack = jnp.concatenate([taps(d, w), taps(d, w + 1)], axis=1)
            acc[:, :K] += lax.dot_general(
                vol, stack, (((1,), (1,)), ((), ())), preferred_element_type=F32
            )

        @pl.when(d < GL)
        def _():
            part = d
            rows = pl.ds(part * GS, GS)
            chain_copy(0, part).wait_recv()
            gsend[2, rows] = own(2, part) + mrecv[0, rows]
            chain_copy(1, part).start()
            chain_copy(3, part).wait_recv()
            gsend[5, rows] = own(5, part) + precv[0, rows]
            chain_copy(4, part).start()

    for part in range(ND):
        ksp[part] = acc[:, part * H : (part + 1) * H]
    for r in range(1, ND):
        kd_copy(r).start()
    kd[k] = ksp[k]

    @pl.loop(0, GL)
    def _(g):
        rows = pl.ds(g * GS, GS)
        chain_copy(4, g).wait_recv()
        gsend[6, rows] = own(6, g) + precv[1, rows]
        chain_copy(5, g).start()
        chain_copy(1, g).wait_recv()
        gsend[1, rows] = own(1, g) + mrecv[1, rows]
        chain_copy(2, g).start()

    def total_of(ref, count):
        value = ref[0]
        for i in range(1, count):
            value = value + ref[i]
        return value

    for r in range(1, ND):
        kd_copy(r).wait_recv()
    value = total_of(kd, ND)
    ksp[ND] = value
    ky[y] = value
    for r in range(1, NY):
        ky_copy(r).start()
    for r in range(1, NY):
        ky_copy(r).wait_recv()
    value = total_of(ky, NY)
    ksp[ND + 1] = value
    kz[z] = value
    for r in range(1, NZ):
        kz_copy(r).start()
    for r in range(1, NZ):
        kz_copy(r).wait_recv()
    value = total_of(kz, NZ)
    ksp[ND + 2] = value
    kf[k] = value
    for r in range(1, ND):
        kf_copy(r).start()

    @pl.loop(0, GL)
    def _(g):
        rows = pl.ds(g * GS, GS)
        chain_copy(2, g).wait_recv()
        chain_copy(5, g).wait_recv()
        total = grx[rows, D : D + W] + mrecv[2, rows] + precv[2, rows]
        gr_out[rows] = (total * (1.0 / GS)).astype(BF16)

    for r in range(1, ND):
        kf_copy(r).wait_recv()
    ks_out[...] = kf[...]

    for i in range(8):
        halo_copy(i).wait_send()

    @pl.loop(0, GL)
    def _(g):
        for step in range(6):
            right_copy(step, g).wait_send()
            chain_copy(step, g).wait_send()

    @pl.loop(0, DL)
    def _(d):
        for r in range(1, ND):
            gv_copy(r, d).wait_send()
        for part in range(ND):
            others(part, lambda: vo_copy(part, d).wait_send())

    for r in range(1, ND):
        kd_copy(r).wait_send()
        kz_copy(r).wait_send()
        kf_copy(r).wait_send()
    for r in range(1, NY):
        ky_copy(r).wait_send()


S_RIGHT = 8
S_GV = S_RIGHT + 6 * GL
S_VO = S_GV + (ND - 1) * DL
S_CHAIN = S_VO + ND * DL
S_KD = S_CHAIN + 6 * GL
S_KY = S_KD + ND - 1
S_KZ = S_KY + NY - 1
S_KF = S_KZ + NZ - 1
N_SENDS = S_KF + ND - 1


def finish(gl_in, gr_in, ks_in, gl_out, gr_out, ks_out, ksv, sems):
    copies = [
        pltpu.make_async_copy(gl_in, gl_out, sems.at[0]),
        pltpu.make_async_copy(gr_in, gr_out, sems.at[1]),
    ]
    for copy in copies:
        copy.start()
    cells = D * NCOL * W * H
    for part in range(ND):
        rows = min(H, K - part * H)
        if rows <= 0:
            break
        square = jnp.concatenate([ks_in[part], jnp.zeros((H - G, H), F32)], axis=0)
        flipped = jnp.transpose(square) * (1.0 / math.sqrt(cells))
        ksv[part * H : part * H + rows] = flipped[:rows, :G]
    last = pltpu.make_async_copy(ksv, ks_out, sems.at[2])
    last.start()
    for copy in copies + [last]:
        copy.wait()


def body(left, right, kernel_weights, cotangent):
    weights = kernel_weights.reshape(K, G)
    vmem = pl.BlockSpec(memory_space=pltpu.VMEM)
    hbm = pl.BlockSpec(memory_space=pltpu.HBM)
    half = lambda *shape: pltpu.VMEM(shape, BF16)
    full = lambda *shape: pltpu.VMEM(shape, F32)
    left_grad, right_grad, parts = pl.pallas_call(
        kernel,
        out_shape=(
            jax.ShapeDtypeStruct((CL, W, H), BF16),
            jax.ShapeDtypeStruct((CL, W, H), BF16),
            jax.ShapeDtypeStruct((ND, G, H), F32),
        ),
        in_specs=[hbm, hbm, hbm, hbm],
        out_specs=(vmem, vmem, vmem),
        scratch_shapes=[
            half(O, DL, W, H),
            full(O * W, H),
            half(K, G),
            half(G, K),
            half(2, DL, O, H),
            half(2, W, O, H),
            half(4, O, H),
            half(DL + 2, W + 2, 3 * O, H),
            half(CL, W, H),
            half(REACH + 1, CL, W, H),
            full(CL, D + W, H),
            full(CL, W, H),
            half(ND, DL, GL, W, H),
            half(ND, DL, GL, W, H),
            half(ND, DL, GL, W, H),
            half(ND, DL, GL, W, H),
            full(DL, W * G, H),
            full(W * G, H),
            full(CL, D + W, H),
            full(REACH + 1, CL, W, H),
            full(3, CL, W, H),
            full(3, CL, W, H),
            full(G, ND * H),
            full(ND + 3, G, H),
            full(ND, G, H),
            full(NY, G, H),
            full(NZ, G, H),
            full(ND, G, H),
            pltpu.SemaphoreType.DMA((4,)),
            pltpu.SemaphoreType.DMA((N_SENDS,)),
            pltpu.SemaphoreType.DMA((N_SENDS,)),
        ],
        compiler_params=pltpu.CompilerParams(
            collective_id=0, has_side_effects=True, vmem_limit_bytes=48 * 1024 * 1024
        ),
    )(*[pltpu.with_memory_space_constraint(a, pltpu.HBM) for a in (cotangent, weights, left, right)])
    left_out, right_out, sums = pl.pallas_call(
        finish,
        out_shape=(
            jax.ShapeDtypeStruct((CL, W, H), BF16),
            jax.ShapeDtypeStruct((CL, W, H), BF16),
            jax.ShapeDtypeStruct((K, G), F32),
        ),
        in_specs=[vmem, vmem, vmem],
        out_specs=(hbm, hbm, hbm),
        scratch_shapes=[full(K, G), pltpu.SemaphoreType.DMA((3,))],
        compiler_params=pltpu.CompilerParams(vmem_limit_bytes=48 * 1024 * 1024),
    )(left_grad, right_grad, parts)
    return (left_out, right_out, sums.reshape(3, 3, 3, O, G))


def solution(mesh):
    return jax.shard_map(
        body,
        mesh=mesh,
        in_specs=(P(None, "col", None), P(None, "col", None), P(), P(None, "disp", "col", None)),
        out_specs=(P("disp", "col", None), P("disp", "col", None), P()),
        check_vma=False,
    )
```

```python
import math

import jax
import jax.numpy as jnp
from jax import lax
from jax.experimental import pallas as pl
from jax.experimental.pallas import tpu as pltpu
from jax.sharding import PartitionSpec as P

C = 320
G = 40
D = 48
O = 32
NCOL = 32
NY = 4
NZ = 8
ND = 8
DL = D // ND
CL = C // ND
GL = G // ND
GS = C // G
W = 8
H = 128
REACH = 6
K = 27 * O
F32 = jnp.float32
BF16 = jnp.bfloat16


def kernel(
    cot_hbm, wgt_hbm, left_hbm, right_hbm,
    gl_out, gr_out, ks_out,
    cotv, ctmp, wgt_in, wgt, halo_w, halo_d, halo_c, e3, lb, rb, rx, lf,
    gvt, gvr, vot, vor, tmp, vtmp, grx, gsend, mrecv, precv,
    acc, ksp, kd, ky, kz, kf,
    local_sems, send_sems, recv_sems,
):
    c = lax.axis_index("col")
    k = lax.axis_index("disp")
    y = c // NZ
    z = c % NZ

    def at(dc=0, dk=0):
        return {"col": (c + dc + NCOL) % NCOL, "disp": (k + dk + ND) % ND}

    def zpeer(r):
        return {"col": y * NZ + (z + r) % NZ, "disp": k}

    def ypeer(r):
        return {"col": ((y + r) % NY) * NZ + z, "disp": k}

    barrier = pltpu.get_barrier_semaphore()
    peers = [at(0, r) for r in range(1, ND)]
    peers += [at(dc, dk) for dc in (-1, 1) for dk in (-1, 0, 1)]
    peers += [at(6, 0), at(-6, 0)]
    peers += [ypeer(r) for r in range(1, NY)]
    for peer in peers:
        pl.semaphore_signal(barrier, inc=1, device_id=peer, device_id_type=pl.DeviceIdType.MESH)

    def copy_of(src, dst, slot, peer, recv_slot=None):
        return pltpu.make_async_remote_copy(
            src_ref=src,
            dst_ref=dst,
            send_sem=send_sems.at[slot],
            recv_sem=recv_sems.at[slot if recv_slot is None else recv_slot],
            device_id=peer,
            device_id_type=pl.DeviceIdType.MESH,
        )

    ALL = pl.ds(1, DL)
    COLS = pl.ds(1, W)

    def own_rows(d, w):
        return e3.at[d, w, pl.ds(O, O)]

    def halo_copy(i):
        return (
            lambda: copy_of(own_rows(ALL, W), halo_w.at[0], 0, at(1, 0)),
            lambda: copy_of(own_rows(ALL, 1), halo_w.at[1], 1, at(-1, 0)),
            lambda: copy_of(own_rows(DL, COLS), halo_d.at[0], 2, at(0, 1)),
            lambda: copy_of(own_rows(1, COLS), halo_d.at[1], 3, at(0, -1)),
            lambda: copy_of(own_rows(DL, W), halo_c.at[0], 4, at(1, 1)),
            lambda: copy_of(own_rows(DL, 1), halo_c.at[1], 5, at(-1, 1)),
            lambda: copy_of(own_rows(1, W), halo_c.at[2], 6, at(1, -1)),
            lambda: copy_of(own_rows(1, 1), halo_c.at[3], 7, at(-1, -1)),
        )[i]()

    def right_copy(step, g):
        src, dst, hop = ((0, 1, 1), (1, 2, 1), (2, 3, 1), (0, 6, 6), (6, 5, -1), (5, 4, -1))[step]
        rows = pl.ds(g * GS, GS)
        source = rb.at[src, rows] if src else right_hbm.at[pl.ds(k * CL + g * GS, GS)]
        return copy_of(source, rb.at[dst, rows], S_RIGHT + step * GL + g, at(hop, 0))

    def gv_copy(r, d):
        return copy_of(gvt.at[(k + r) % ND, d], gvr.at[k, d], S_GV + (r - 1) * DL + d, at(0, r))

    def vo_copy(part, d):
        return copy_of(
            vot.at[part, d], vor.at[k, d], S_VO + part * DL + d, at_disp(part), S_VO + k * DL + d
        )

    def vo_arrival(part, d):
        return copy_of(
            vot.at[part, d], vor.at[part, d], S_VO + part * DL + d, at_disp(part)
        )

    def at_disp(part):
        return {"col": c, "disp": part}

    def others(part, act):
        @pl.when(k != part)
        def _():
            act()

    def chain_copy(step, g):
        src, recv, slot, hop = (
            (4, mrecv, 0, -1), (3, mrecv, 1, -1), (2, mrecv, 2, -1), (1, mrecv, 3, -1),
            (5, precv, 0, 1), (6, precv, 1, -6),
        )[step]
        rows = pl.ds(g * GS, GS)
        return copy_of(
            gsend.at[src, rows], recv.at[slot, rows], S_CHAIN + step * GL + g, at(hop, 0)
        )

    def kd_copy(r):
        return copy_of(ksp.at[(k + r) % ND], kd.at[k], S_KD + r - 1, at(0, r))

    def ky_copy(r):
        return copy_of(ksp.at[ND], ky.at[y], S_KY + r - 1, ypeer(r))

    def kz_copy(r):
        return copy_of(ksp.at[ND + 1], kz.at[z], S_KZ + r - 1, zpeer(r))

    def kf_copy(r):
        return copy_of(ksp.at[ND + 2], kf.at[k], S_KF + r - 1, at(0, r))

    lane = lax.broadcasted_iota(jnp.int32, (O, H), 1)

    def spread(value, d, w):
        above = jnp.where(lane == H - 1, 0.0, pltpu.roll(value, H - 1, 1))
        below = jnp.where(lane == 0, 0.0, pltpu.roll(value, 1, 1))
        e3[d, w, 0:O] = above.astype(BF16)
        e3[d, w, O : 2 * O] = value.astype(BF16)
        e3[d, w, 2 * O : 3 * O] = below.astype(BF16)

    local_cot = pltpu.make_async_copy(cot_hbm, cotv, local_sems.at[2])
    local_right = pltpu.make_async_copy(right_hbm.at[pl.ds(k * CL, CL)], rb.at[0], local_sems.at[0])
    local_left = pltpu.make_async_copy(left_hbm.at[pl.ds(k * CL, CL)], lb, local_sems.at[1])
    local_wgt = pltpu.make_async_copy(wgt_hbm, wgt_in, local_sems.at[3])
    local_cot.start()
    local_wgt.start()
    local_right.start()
    local_left.start()
    local_cot.wait()

    @pl.loop(0, DL)
    def _(d):
        for o in range(O):
            ctmp[o * W : (o + 1) * W] = cotv[o, d].astype(F32)
        for w in range(W):
            spread(ctmp[pl.ds(w, O, stride=W)], d + 1, w + 1)

    pl.semaphore_wait(barrier, len(peers))
    for i in range(8):
        halo_copy(i).start()

    @pl.loop(0, GL)
    def _(g):
        right_copy(3, g).start()
        right_copy(0, g).start()

    eye = (
        lax.broadcasted_iota(jnp.int32, (G, G), 0) == lax.broadcasted_iota(jnp.int32, (G, G), 1)
    ).astype(F32)
    local_wgt.wait()
    wgt[...] = lax.dot_general(
        eye.astype(BF16), wgt_in[...], (((1,), (1,)), ((), ())), preferred_element_type=F32
    ).astype(BF16)
    local_left.wait()
    lf[...] = lb[...].astype(F32)
    local_right.wait()

    def hand_on(step, first=0, last=GL):
        @pl.loop(first, last)
        def _(g):
            right_copy(step, g).wait_recv()
            right_copy(step + 1, g).start()

    def taps(d, w):
        return jnp.concatenate(
            [e3[d + 2 - p, w + 2 - q] for p in range(3) for q in range(3)], axis=0
        )

    def products(first, last, pairs):
        @pl.loop(first, last)
        def _(d):
            for a, b in pairs:
                stack = jnp.concatenate([taps(d, a), taps(d, b)], axis=1)
                out = jnp.dot(wgt[...], stack, preferred_element_type=F32)
                tmp[d, a * G : (a + 1) * G] = out[:, :H]
                tmp[d, b * G : (b + 1) * G] = out[:, H:]

    def finish_levels(first, last):
        products(first, last, ((0, W - 1),))

        @pl.loop(first, last)
        def _(d):
            for g in range(G):
                gvt[g // GL, d, g % GL] = tmp[d, pl.ds(g, W, stride=G)].astype(BF16)
            for r in range(1, ND):
                gv_copy(r, d).start()

    inner = ((1, 2), (3, 4), (5, 6))
    products(1, DL - 1, inner)

    lo_c, hi_c, lo_k, hi_k = (c > 0, c < NCOL - 1, k > 0, k < ND - 1)

    def border(block, ok, d, w):
        spread(jnp.where(ok, block.astype(F32), 0.0), d, w)

    for i in range(2, 4):
        halo_copy(i).wait_recv()

    @pl.loop(0, W)
    def _(w):
        border(halo_d[0, w], lo_k, 0, w + 1)
        border(halo_d[1, w], hi_k, DL + 1, w + 1)

    hand_on(0, 0, 3)
    products(0, 1, inner)
    products(DL - 1, DL, inner)
    hand_on(0, 3)
    for i in range(2):
        halo_copy(i).wait_recv()

    @pl.loop(0, DL)
    def _(d):
        border(halo_w[0, d], lo_c, d + 1, 0)
        border(halo_w[1, d], hi_c, d + 1, W + 1)

    for i in range(4, 8):
        halo_copy(i).wait_recv()
    border(halo_c[0], lo_c & lo_k, 0, 0)
    border(halo_c[1], hi_c & lo_k, 0, W + 1)
    border(halo_c[2], lo_c & hi_k, DL + 1, 0)
    border(halo_c[3], hi_c & hi_k, DL + 1, W + 1)

    hand_on(3)
    finish_levels(0, 3)
    hand_on(1)
    finish_levels(3, DL)
    hand_on(4)
    gvr[k] = gvt[k]

    def widen(g, blocks):
        rows = pl.ds(g * GS, GS)
        for j in blocks:
            block = rb[j, rows].astype(F32)
            if j:
                block = jnp.where(c >= j, block, 0.0)
            rx[rows, D - W * j : D - W * j + W] = block

    def volume(parts):
        for level in range(DL):

            @pl.loop(0, GL)
            def _(g):
                for part in parts:
                    d = part * DL + level
                    total = None
                    for i in range(GS):
                        term = lf[g * GS + i] * rx[g * GS + i, D - d : D - d + W]
                        total = term if total is None else total + term
                    vot[part, level, g] = (total * (1.0 / GS)).astype(BF16)

            for part in parts:
                others(part, lambda: vo_copy(part, level).start())

    @pl.loop(0, GL)
    def _(g):
        right_copy(2, g).wait_recv()
        widen(g, (0, 1, 2, 3))

    volume((0, 1, 2, 3))

    @pl.loop(0, GL)
    def _(g):
        right_copy(5, g).wait_recv()
        widen(g, (4, 5, 6))

    volume((4, 5, 6, 7))
    vor[k] = vot[k]

    @pl.loop(0, DL)
    def _(d):
        for r in range(1, ND):
            gv_copy(r, d).wait_recv()

    def own(j, g):
        return jnp.where(c >= j, grx[pl.ds(g * GS, GS), D - W * j : D - W * j + W], 0.0)

    @pl.loop(0, GL)
    def _(g):
        rows = pl.ds(g * GS, GS)
        grx[rows] = jnp.zeros((GS, D + W, H), F32)
        sums = [jnp.zeros((W, H), F32) for _ in range(GS)]
        for d in range(D):
            grad = gvr[d // DL, d % DL, g].astype(F32)
            for i in range(GS):
                ch = g * GS + i
                sums[i] = sums[i] + grad * rx[ch, D - d : D - d + W]
                grx[ch, D - d : D - d + W] += grad * lf[ch]
        gsend[5, rows] = own(5, g)
        gsend[4, rows] = own(4, g)
        chain_copy(4, g).start()
        chain_copy(0, g).start()
        for i in range(GS):
            gl_out[g * GS + i] = (sums[i] * (1.0 / GS)).astype(BF16)

    def pass_on(part):
        rows = pl.ds(part * GS, GS)
        chain_copy(4, part).wait_recv()
        gsend[6, rows] = own(6, part) + precv[0, rows]
        chain_copy(5, part).start()
        chain_copy(0, part).wait_recv()
        gsend[3, rows] = own(3, part) + mrecv[0, rows]
        chain_copy(1, part).start()

    acc[...] = jnp.zeros_like(acc)

    @pl.loop(0, DL)
    def _(d):
        for part in range(ND):
            others(part, lambda: vo_arrival(part, d).wait_recv())
        for part in range(ND):
            for g in range(GL):
                vtmp[(part * GL + g) * W : (part * GL + g + 1) * W] = vor[part, d, g].astype(F32)
        for w in range(0, W, 2):
            vol = jnp.concatenate(
                [vtmp[pl.ds(w, G, stride=W)], vtmp[pl.ds(w + 1, G, stride=W)]], axis=1
            ).astype(BF16)
            stack = jnp.concatenate([taps(d, w), taps(d, w + 1)], axis=1)
            acc[:, :K] += lax.dot_general(
                vol, stack, (((1,), (1,)), ((), ())), preferred_element_type=F32
            )

        @pl.when(d >= 2)
        def _():
            pass_on(d - 2)

    for part in range(ND):
        ksp[part] = acc[:, part * H : (part + 1) * H]
    for r in range(1, ND):
        kd_copy(r).start()
    kd[k] = ksp[k]
    for part in range(4, GL):
        pass_on(part)

    def add_on(j):
        @pl.loop(0, GL)
        def _(g):
            rows = pl.ds(g * GS, GS)
            chain_copy(3 - j, g).wait_recv()
            gsend[j, rows] = own(j, g) + mrecv[3 - j, rows]
            chain_copy(4 - j, g).start()

    def total_of(ref, count):
        value = ref[0]
        for i in range(1, count):
            value = value + ref[i]
        return value

    for r in range(1, ND):
        kd_copy(r).wait_recv()
    value = total_of(kd, ND)
    ksp[ND] = value
    ky[y] = value
    for r in range(1, NY):
        ky_copy(r).start()
    add_on(2)
    for r in range(1, NY):
        ky_copy(r).wait_recv()
    value = total_of(ky, NY)
    ksp[ND + 1] = value
    kz[z] = value
    for r in range(1, NZ):
        kz_copy(r).start()
    add_on(1)
    for r in range(1, NZ):
        kz_copy(r).wait_recv()
    value = total_of(kz, NZ)
    ksp[ND + 2] = value
    kf[k] = value
    for r in range(1, ND):
        kf_copy(r).start()

    @pl.loop(0, GL)
    def _(g):
        rows = pl.ds(g * GS, GS)
        chain_copy(3, g).wait_recv()
        chain_copy(5, g).wait_recv()
        total = grx[rows, D : D + W] + mrecv[3, rows] + precv[1, rows]
        gr_out[rows] = (total * (1.0 / GS)).astype(BF16)

    for r in range(1, ND):
        kf_copy(r).wait_recv()
    ks_out[...] = kf[...]

    for i in range(8):
        halo_copy(i).wait_send()

    @pl.loop(0, GL)
    def _(g):
        for step in range(6):
            right_copy(step, g).wait_send()
            chain_copy(step, g).wait_send()

    @pl.loop(0, DL)
    def _(d):
        for r in range(1, ND):
            gv_copy(r, d).wait_send()
        for part in range(ND):
            others(part, lambda: vo_copy(part, d).wait_send())

    for r in range(1, ND):
        kd_copy(r).wait_send()
        kz_copy(r).wait_send()
        kf_copy(r).wait_send()
    for r in range(1, NY):
        ky_copy(r).wait_send()


S_RIGHT = 8
S_GV = S_RIGHT + 6 * GL
S_VO = S_GV + (ND - 1) * DL
S_CHAIN = S_VO + ND * DL
S_KD = S_CHAIN + 6 * GL
S_KY = S_KD + ND - 1
S_KZ = S_KY + NY - 1
S_KF = S_KZ + NZ - 1
N_SENDS = S_KF + ND - 1


def finish(gl_in, gr_in, ks_in, gl_out, gr_out, ks_out, ksv, sems):
    copies = [
        pltpu.make_async_copy(gl_in, gl_out, sems.at[0]),
        pltpu.make_async_copy(gr_in, gr_out, sems.at[1]),
    ]
    for copy in copies:
        copy.start()
    cells = D * NCOL * W * H
    for part in range(ND):
        rows = min(H, K - part * H)
        if rows <= 0:
            break
        square = jnp.concatenate([ks_in[part], jnp.zeros((H - G, H), F32)], axis=0)
        flipped = jnp.transpose(square) * (1.0 / math.sqrt(cells))
        ksv[part * H : part * H + rows] = flipped[:rows, :G]
    last = pltpu.make_async_copy(ksv, ks_out, sems.at[2])
    last.start()
    for copy in copies + [last]:
        copy.wait()


def body(left, right, kernel_weights, cotangent):
    weights = kernel_weights.reshape(K, G)
    vmem = pl.BlockSpec(memory_space=pltpu.VMEM)
    hbm = pl.BlockSpec(memory_space=pltpu.HBM)
    half = lambda *shape: pltpu.VMEM(shape, BF16)
    full = lambda *shape: pltpu.VMEM(shape, F32)
    left_grad, right_grad, parts = pl.pallas_call(
        kernel,
        out_shape=(
            jax.ShapeDtypeStruct((CL, W, H), BF16),
            jax.ShapeDtypeStruct((CL, W, H), BF16),
            jax.ShapeDtypeStruct((ND, G, H), F32),
        ),
        in_specs=[hbm, hbm, hbm, hbm],
        out_specs=(vmem, vmem, vmem),
        scratch_shapes=[
            half(O, DL, W, H),
            full(O * W, H),
            half(K, G),
            half(G, K),
            half(2, DL, O, H),
            half(2, W, O, H),
            half(4, O, H),
            half(DL + 2, W + 2, 3 * O, H),
            half(CL, W, H),
            half(REACH + 1, CL, W, H),
            full(CL, D + W, H),
            full(CL, W, H),
            half(ND, DL, GL, W, H),
            half(ND, DL, GL, W, H),
            half(ND, DL, GL, W, H),
            half(ND, DL, GL, W, H),
            full(DL, W * G, H),
            full(W * G, H),
            full(CL, D + W, H),
            full(REACH + 1, CL, W, H),
            full(4, CL, W, H),
            full(2, CL, W, H),
            full(G, ND * H),
            full(ND + 3, G, H),
            full(ND, G, H),
            full(NY, G, H),
            full(NZ, G, H),
            full(ND, G, H),
            pltpu.SemaphoreType.DMA((4,)),
            pltpu.SemaphoreType.DMA((N_SENDS,)),
            pltpu.SemaphoreType.DMA((N_SENDS,)),
        ],
        compiler_params=pltpu.CompilerParams(
            collective_id=0, has_side_effects=True, vmem_limit_bytes=48 * 1024 * 1024
        ),
    )(*[pltpu.with_memory_space_constraint(a, pltpu.HBM) for a in (cotangent, weights, left, right)])
    left_out, right_out, sums = pl.pallas_call(
        finish,
        out_shape=(
            jax.ShapeDtypeStruct((CL, W, H), BF16),
            jax.ShapeDtypeStruct((CL, W, H), BF16),
            jax.ShapeDtypeStruct((K, G), F32),
        ),
        in_specs=[vmem, vmem, vmem],
        out_specs=(hbm, hbm, hbm),
        scratch_shapes=[full(K, G), pltpu.SemaphoreType.DMA((3,))],
        compiler_params=pltpu.CompilerParams(vmem_limit_bytes=48 * 1024 * 1024),
    )(left_grad, right_grad, parts)
    return (left_out, right_out, sums.reshape(3, 3, 3, O, G))


def solution(mesh):
    return jax.shard_map(
        body,
        mesh=mesh,
        in_specs=(P(None, "col", None), P(None, "col", None), P(), P(None, "disp", "col", None)),
        out_specs=(P("disp", "col", None), P("disp", "col", None), P()),
        check_vma=False,
    )
```

```python
import math

import jax
import jax.numpy as jnp
from jax import lax
from jax.experimental import pallas as pl
from jax.experimental.pallas import tpu as pltpu
from jax.sharding import PartitionSpec as P

C = 320
G = 40
D = 48
O = 32
NCOL = 32
NY = 4
NZ = 8
ND = 8
DL = D // ND
CL = C // ND
GL = G // ND
GS = C // G
W = 8
H = 128
FAR_FIRST = (4, 3, 5, 2, 6, 1, 7)
REACH = 6
K = 27 * O
F32 = jnp.float32
BF16 = jnp.bfloat16


def kernel(
    cot_hbm, wgt_hbm, left_hbm, right_hbm,
    gl_out, gr_out, ks_out,
    cotv, ctmp, wgt_in, wgt, halo_w, halo_d, halo_c, e3, lb, rb, rx, lf,
    gvt, gvr, vot, vor, tmp, vtmp, grx, gsend, mrecv, precv,
    acc, ksp, kd, ky, kz, kf,
    local_sems, send_sems, recv_sems,
):
    c = lax.axis_index("col")
    k = lax.axis_index("disp")
    y = c // NZ
    z = c % NZ

    def at(dc=0, dk=0):
        return {"col": (c + dc + NCOL) % NCOL, "disp": (k + dk + ND) % ND}

    def zpeer(r):
        return {"col": y * NZ + (z + r) % NZ, "disp": k}

    def ypeer(r):
        return {"col": ((y + r) % NY) * NZ + z, "disp": k}

    barrier = pltpu.get_barrier_semaphore()
    peers = [at(0, r) for r in range(1, ND)]
    peers += [at(dc, dk) for dc in (-1, 1) for dk in (-1, 0, 1)]
    peers += [at(6, 0), at(-6, 0)]
    peers += [ypeer(r) for r in range(1, NY)]
    for peer in peers:
        pl.semaphore_signal(barrier, inc=1, device_id=peer, device_id_type=pl.DeviceIdType.MESH)

    def copy_of(src, dst, slot, peer, recv_slot=None):
        return pltpu.make_async_remote_copy(
            src_ref=src,
            dst_ref=dst,
            send_sem=send_sems.at[slot],
            recv_sem=recv_sems.at[slot if recv_slot is None else recv_slot],
            device_id=peer,
            device_id_type=pl.DeviceIdType.MESH,
        )

    ALL = pl.ds(1, DL)
    COLS = pl.ds(1, W)

    def own_rows(d, w):
        return e3.at[d, w, pl.ds(O, O)]

    def halo_copy(i):
        return (
            lambda: copy_of(own_rows(ALL, W), halo_w.at[0], 0, at(1, 0)),
            lambda: copy_of(own_rows(ALL, 1), halo_w.at[1], 1, at(-1, 0)),
            lambda: copy_of(own_rows(DL, COLS), halo_d.at[0], 2, at(0, 1)),
            lambda: copy_of(own_rows(1, COLS), halo_d.at[1], 3, at(0, -1)),
            lambda: copy_of(own_rows(DL, W), halo_c.at[0], 4, at(1, 1)),
            lambda: copy_of(own_rows(DL, 1), halo_c.at[1], 5, at(-1, 1)),
            lambda: copy_of(own_rows(1, W), halo_c.at[2], 6, at(1, -1)),
            lambda: copy_of(own_rows(1, 1), halo_c.at[3], 7, at(-1, -1)),
        )[i]()

    def right_copy(step, g):
        src, dst, hop = ((0, 1, 1), (1, 2, 1), (2, 3, 1), (0, 6, 6), (6, 5, -1), (5, 4, -1))[step]
        rows = pl.ds(g * GS, GS)
        source = rb.at[src, rows] if src else right_hbm.at[pl.ds(k * CL + g * GS, GS)]
        return copy_of(source, rb.at[dst, rows], S_RIGHT + step * GL + g, at(hop, 0))

    def gv_copy(r, d):
        return copy_of(gvt.at[(k + r) % ND, d], gvr.at[k, d], S_GV + (r - 1) * DL + d, at(0, r))

    def vo_copy(part, d):
        return copy_of(
            vot.at[part, d], vor.at[k, d], S_VO + part * DL + d, at_disp(part), S_VO + k * DL + d
        )

    def vo_arrival(part, d):
        return copy_of(
            vot.at[part, d], vor.at[part, d], S_VO + part * DL + d, at_disp(part)
        )

    def at_disp(part):
        return {"col": c, "disp": part}

    def others(part, act):
        @pl.when(k != part)
        def _():
            act()

    def chain_copy(step, g):
        src, recv, slot, hop = (
            (4, mrecv, 0, -1), (3, mrecv, 1, -1), (2, mrecv, 2, -1), (1, mrecv, 3, -1),
            (5, precv, 0, 1), (6, precv, 1, -6),
        )[step]
        rows = pl.ds(g * GS, GS)
        return copy_of(
            gsend.at[src, rows], recv.at[slot, rows], S_CHAIN + step * GL + g, at(hop, 0)
        )

    def kd_copy(r):
        return copy_of(ksp.at[(k + r) % ND], kd.at[k], S_KD + r - 1, at(0, r))

    def ky_copy(r):
        return copy_of(ksp.at[ND], ky.at[y], S_KY + r - 1, ypeer(r))

    def kz_copy(r):
        return copy_of(ksp.at[ND + 1], kz.at[z], S_KZ + r - 1, zpeer(r))

    def kf_copy(r):
        return copy_of(ksp.at[ND + 2], kf.at[k], S_KF + r - 1, at(0, r))

    lane = lax.broadcasted_iota(jnp.int32, (O, H), 1)

    def spread(value, d, w):
        above = jnp.where(lane == H - 1, 0.0, pltpu.roll(value, H - 1, 1))
        below = jnp.where(lane == 0, 0.0, pltpu.roll(value, 1, 1))
        e3[d, w, 0:O] = above.astype(BF16)
        e3[d, w, O : 2 * O] = value.astype(BF16)
        e3[d, w, 2 * O : 3 * O] = below.astype(BF16)

    local_cot = pltpu.make_async_copy(cot_hbm, cotv, local_sems.at[2])
    local_right = pltpu.make_async_copy(right_hbm.at[pl.ds(k * CL, CL)], rb.at[0], local_sems.at[0])
    local_left = pltpu.make_async_copy(left_hbm.at[pl.ds(k * CL, CL)], lb, local_sems.at[1])
    local_wgt = pltpu.make_async_copy(wgt_hbm, wgt_in, local_sems.at[3])
    local_cot.start()
    local_wgt.start()
    local_right.start()
    local_left.start()
    local_cot.wait()

    @pl.loop(0, DL)
    def _(d):
        for o in range(O):
            ctmp[o * W : (o + 1) * W] = cotv[o, d].astype(F32)
        for w in range(W):
            spread(ctmp[pl.ds(w, O, stride=W)], d + 1, w + 1)

    pl.semaphore_wait(barrier, len(peers))
    for i in range(8):
        halo_copy(i).start()

    @pl.loop(0, GL)
    def _(g):
        right_copy(3, g).start()
        right_copy(0, g).start()

    eye = (
        lax.broadcasted_iota(jnp.int32, (G, G), 0) == lax.broadcasted_iota(jnp.int32, (G, G), 1)
    ).astype(F32)
    local_wgt.wait()
    wgt[...] = lax.dot_general(
        eye.astype(BF16), wgt_in[...], (((1,), (1,)), ((), ())), preferred_element_type=F32
    ).astype(BF16)
    local_left.wait()
    lf[...] = lb[...].astype(F32)
    local_right.wait()

    def hand_on(step, first=0, last=GL):
        @pl.loop(first, last)
        def _(g):
            right_copy(step, g).wait_recv()
            right_copy(step + 1, g).start()

    def taps(d, w):
        return jnp.concatenate(
            [e3[d + 2 - p, w + 2 - q] for p in range(3) for q in range(3)], axis=0
        )

    def products(first, last, pairs):
        @pl.loop(first, last)
        def _(d):
            for a, b in pairs:
                stack = jnp.concatenate([taps(d, a), taps(d, b)], axis=1)
                out = jnp.dot(wgt[...], stack, preferred_element_type=F32)
                tmp[d, a * G : (a + 1) * G] = out[:, :H]
                tmp[d, b * G : (b + 1) * G] = out[:, H:]

    def finish_levels(first, last):
        products(first, last, ((0, W - 1),))

        @pl.loop(first, last)
        def _(d):
            for g in range(G):
                gvt[g // GL, d, g % GL] = tmp[d, pl.ds(g, W, stride=G)].astype(BF16)
            for r in range(1, ND):
                gv_copy(r, d).start()

    inner = ((1, 2), (3, 4), (5, 6))
    products(1, DL - 1, inner)

    lo_c, hi_c, lo_k, hi_k = (c > 0, c < NCOL - 1, k > 0, k < ND - 1)

    def border(block, ok, d, w):
        spread(jnp.where(ok, block.astype(F32), 0.0), d, w)

    for i in range(2, 4):
        halo_copy(i).wait_recv()

    @pl.loop(0, W)
    def _(w):
        border(halo_d[0, w], lo_k, 0, w + 1)
        border(halo_d[1, w], hi_k, DL + 1, w + 1)

    hand_on(0, 0, 3)
    products(0, 1, inner)
    products(DL - 1, DL, inner)
    hand_on(0, 3)
    for i in range(2):
        halo_copy(i).wait_recv()

    @pl.loop(0, DL)
    def _(d):
        border(halo_w[0, d], lo_c, d + 1, 0)
        border(halo_w[1, d], hi_c, d + 1, W + 1)

    for i in range(4, 8):
        halo_copy(i).wait_recv()
    border(halo_c[0], lo_c & lo_k, 0, 0)
    border(halo_c[1], hi_c & lo_k, 0, W + 1)
    border(halo_c[2], lo_c & hi_k, DL + 1, 0)
    border(halo_c[3], hi_c & hi_k, DL + 1, W + 1)

    hand_on(3)
    finish_levels(0, 3)
    hand_on(1)
    finish_levels(3, DL)
    hand_on(4)
    gvr[k] = gvt[k]

    def widen(g, blocks):
        rows = pl.ds(g * GS, GS)
        for j in blocks:
            block = rb[j, rows].astype(F32)
            if j:
                block = jnp.where(c >= j, block, 0.0)
            rx[rows, D - W * j : D - W * j + W] = block

    def volume(parts):
        for level in range(DL):

            @pl.loop(0, GL)
            def _(g):
                for part in parts:
                    d = part * DL + level
                    total = None
                    for i in range(GS):
                        term = lf[g * GS + i] * rx[g * GS + i, D - d : D - d + W]
                        total = term if total is None else total + term
                    vot[part, level, g] = (total * (1.0 / GS)).astype(BF16)

            for part in parts:
                others(part, lambda: vo_copy(part, level).start())

    @pl.loop(0, GL)
    def _(g):
        right_copy(2, g).wait_recv()
        widen(g, (0, 1, 2, 3))

    volume((0, 1, 2, 3))

    @pl.loop(0, GL)
    def _(g):
        right_copy(5, g).wait_recv()
        widen(g, (4, 5, 6))

    volume((4, 5, 6, 7))
    vor[k] = vot[k]

    @pl.loop(0, DL)
    def _(d):
        for r in range(1, ND):
            gv_copy(r, d).wait_recv()

    def own(j, g):
        return jnp.where(c >= j, grx[pl.ds(g * GS, GS), D - W * j : D - W * j + W], 0.0)

    @pl.loop(0, GL)
    def _(g):
        rows = pl.ds(g * GS, GS)
        grx[rows] = jnp.zeros((GS, D + W, H), F32)
        sums = [jnp.zeros((W, H), F32) for _ in range(GS)]
        for d in range(D):
            grad = gvr[d // DL, d % DL, g].astype(F32)
            for i in range(GS):
                ch = g * GS + i
                sums[i] = sums[i] + grad * rx[ch, D - d : D - d + W]
                grx[ch, D - d : D - d + W] += grad * lf[ch]
        gsend[5, rows] = own(5, g)
        gsend[4, rows] = own(4, g)
        chain_copy(4, g).start()
        chain_copy(0, g).start()
        for i in range(GS):
            gl_out[g * GS + i] = (sums[i] * (1.0 / GS)).astype(BF16)

    def pass_on(part):
        rows = pl.ds(part * GS, GS)
        chain_copy(4, part).wait_recv()
        gsend[6, rows] = own(6, part) + precv[0, rows]
        chain_copy(5, part).start()
        chain_copy(0, part).wait_recv()
        gsend[3, rows] = own(3, part) + mrecv[0, rows]
        chain_copy(1, part).start()

    acc[...] = jnp.zeros_like(acc)

    @pl.loop(0, DL)
    def _(d):
        for part in range(ND):
            others(part, lambda: vo_arrival(part, d).wait_recv())
        for part in range(ND):
            for g in range(GL):
                vtmp[(part * GL + g) * W : (part * GL + g + 1) * W] = vor[part, d, g].astype(F32)
        for w in range(0, W, 2):
            vol = jnp.concatenate(
                [vtmp[pl.ds(w, G, stride=W)], vtmp[pl.ds(w + 1, G, stride=W)]], axis=1
            ).astype(BF16)
            stack = jnp.concatenate([taps(d, w), taps(d, w + 1)], axis=1)
            acc[:, :K] += lax.dot_general(
                vol, stack, (((1,), (1,)), ((), ())), preferred_element_type=F32
            )

        @pl.when(d >= 2)
        def _():
            pass_on(d - 2)

    for part in range(ND):
        ksp[part] = acc[:, part * H : (part + 1) * H]
    for r in FAR_FIRST:
        kd_copy(r).start()
    kd[k] = ksp[k]
    for part in range(4, GL):
        pass_on(part)

    def add_on(j):
        @pl.loop(0, GL)
        def _(g):
            rows = pl.ds(g * GS, GS)
            chain_copy(3 - j, g).wait_recv()
            gsend[j, rows] = own(j, g) + mrecv[3 - j, rows]
            chain_copy(4 - j, g).start()

    def total_of(ref, count):
        value = ref[0]
        for i in range(1, count):
            value = value + ref[i]
        return value

    for r in range(1, ND):
        kd_copy(r).wait_recv()
    value = total_of(kd, ND)
    ksp[ND] = value
    ky[y] = value
    for r in (2, 1, 3):
        ky_copy(r).start()
    add_on(2)
    for r in range(1, NY):
        ky_copy(r).wait_recv()
    value = total_of(ky, NY)
    ksp[ND + 1] = value
    kz[z] = value
    for r in FAR_FIRST:
        kz_copy(r).start()
    add_on(1)
    for r in range(1, NZ):
        kz_copy(r).wait_recv()
    value = total_of(kz, NZ)
    ksp[ND + 2] = value
    kf[k] = value
    for r in FAR_FIRST:
        kf_copy(r).start()

    @pl.loop(0, GL)
    def _(g):
        rows = pl.ds(g * GS, GS)
        chain_copy(3, g).wait_recv()
        chain_copy(5, g).wait_recv()
        total = grx[rows, D : D + W] + mrecv[3, rows] + precv[1, rows]
        gr_out[rows] = (total * (1.0 / GS)).astype(BF16)

    for r in range(1, ND):
        kf_copy(r).wait_recv()
    ks_out[...] = kf[...]

    for i in range(8):
        halo_copy(i).wait_send()

    @pl.loop(0, GL)
    def _(g):
        for step in range(6):
            right_copy(step, g).wait_send()
            chain_copy(step, g).wait_send()

    @pl.loop(0, DL)
    def _(d):
        for r in range(1, ND):
            gv_copy(r, d).wait_send()
        for part in range(ND):
            others(part, lambda: vo_copy(part, d).wait_send())

    for r in range(1, ND):
        kd_copy(r).wait_send()
        kz_copy(r).wait_send()
        kf_copy(r).wait_send()
    for r in range(1, NY):
        ky_copy(r).wait_send()


S_RIGHT = 8
S_GV = S_RIGHT + 6 * GL
S_VO = S_GV + (ND - 1) * DL
S_CHAIN = S_VO + ND * DL
S_KD = S_CHAIN + 6 * GL
S_KY = S_KD + ND - 1
S_KZ = S_KY + NY - 1
S_KF = S_KZ + NZ - 1
N_SENDS = S_KF + ND - 1


def finish(gl_in, gr_in, ks_in, gl_out, gr_out, ks_out, ksv, sems):
    copies = [
        pltpu.make_async_copy(gl_in, gl_out, sems.at[0]),
        pltpu.make_async_copy(gr_in, gr_out, sems.at[1]),
    ]
    for copy in copies:
        copy.start()
    cells = D * NCOL * W * H
    for part in range(ND):
        rows = min(H, K - part * H)
        if rows <= 0:
            break
        square = jnp.concatenate([ks_in[part], jnp.zeros((H - G, H), F32)], axis=0)
        flipped = jnp.transpose(square) * (1.0 / math.sqrt(cells))
        ksv[part * H : part * H + rows] = flipped[:rows, :G]
    last = pltpu.make_async_copy(ksv, ks_out, sems.at[2])
    last.start()
    for copy in copies + [last]:
        copy.wait()


def body(left, right, kernel_weights, cotangent):
    weights = kernel_weights.reshape(K, G)
    vmem = pl.BlockSpec(memory_space=pltpu.VMEM)
    hbm = pl.BlockSpec(memory_space=pltpu.HBM)
    half = lambda *shape: pltpu.VMEM(shape, BF16)
    full = lambda *shape: pltpu.VMEM(shape, F32)
    left_grad, right_grad, parts = pl.pallas_call(
        kernel,
        out_shape=(
            jax.ShapeDtypeStruct((CL, W, H), BF16),
            jax.ShapeDtypeStruct((CL, W, H), BF16),
            jax.ShapeDtypeStruct((ND, G, H), F32),
        ),
        in_specs=[hbm, hbm, hbm, hbm],
        out_specs=(vmem, vmem, vmem),
        scratch_shapes=[
            half(O, DL, W, H),
            full(O * W, H),
            half(K, G),
            half(G, K),
            half(2, DL, O, H),
            half(2, W, O, H),
            half(4, O, H),
            half(DL + 2, W + 2, 3 * O, H),
            half(CL, W, H),
            half(REACH + 1, CL, W, H),
            full(CL, D + W, H),
            full(CL, W, H),
            half(ND, DL, GL, W, H),
            half(ND, DL, GL, W, H),
            half(ND, DL, GL, W, H),
            half(ND, DL, GL, W, H),
            full(DL, W * G, H),
            full(W * G, H),
            full(CL, D + W, H),
            full(REACH + 1, CL, W, H),
            full(4, CL, W, H),
            full(2, CL, W, H),
            full(G, ND * H),
            full(ND + 3, G, H),
            full(ND, G, H),
            full(NY, G, H),
            full(NZ, G, H),
            full(ND, G, H),
            pltpu.SemaphoreType.DMA((4,)),
            pltpu.SemaphoreType.DMA((N_SENDS,)),
            pltpu.SemaphoreType.DMA((N_SENDS,)),
        ],
        compiler_params=pltpu.CompilerParams(
            collective_id=0, has_side_effects=True, vmem_limit_bytes=48 * 1024 * 1024
        ),
    )(*[pltpu.with_memory_space_constraint(a, pltpu.HBM) for a in (cotangent, weights, left, right)])
    left_out, right_out, sums = pl.pallas_call(
        finish,
        out_shape=(
            jax.ShapeDtypeStruct((CL, W, H), BF16),
            jax.ShapeDtypeStruct((CL, W, H), BF16),
            jax.ShapeDtypeStruct((K, G), F32),
        ),
        in_specs=[vmem, vmem, vmem],
        out_specs=(hbm, hbm, hbm),
        scratch_shapes=[full(K, G), pltpu.SemaphoreType.DMA((3,))],
        compiler_params=pltpu.CompilerParams(vmem_limit_bytes=48 * 1024 * 1024),
    )(left_grad, right_grad, parts)
    return (left_out, right_out, sums.reshape(3, 3, 3, O, G))


def solution(mesh):
    return jax.shard_map(
        body,
        mesh=mesh,
        in_specs=(P(None, "col", None), P(None, "col", None), P(), P(None, "disp", "col", None)),
        out_specs=(P("disp", "col", None), P("disp", "col", None), P()),
        check_vma=False,
    )
```
